256 devices in a mesh: dom: 8 (over y, z_hi), row: 32 (over z_lo, x, core).
Axes of the slice: x: 4, y: 4, z: 8 (z_hi: 2, z_lo: 4; z = z_hi * 4 + z_lo), core: 2. Of those that a mesh axis runs over, the one named last changes fastest.
Arguments:
- memory: bfloat16 [524288, 256], P(('dom', 'row')), may hold values from -5 to 5
- node_time: int32 [524288], P(('dom', 'row')), may hold values from 0 to 999
- target: int32 [4, 131072], P(None, ('dom', 'row')), may hold values from -1 to 2047
- source: int32 [4, 131072], P(None, ('dom', 'row')), may hold values from 0 to 131071, as said below
- event_time: int32 [4, 131072], P(None, ('dom', 'row')), may hold values from 1000 to 2999
- edge_feat: bfloat16 [4, 131072, 128], P(None, ('dom', 'row')), may hold values from -5 to 5
- owner_group: int32 [4], replicated, may hold values from 0 to 7
- w_message: bfloat16 [768, 256], replicated, may hold values from -0.21875 to 0.21875
- frequency: float32 [128], replicated, may hold values from 0.001 to 0.1
- phase_shift: float32 [128], replicated, may hold values from -3.140625 to 3.140625
- w_input: bfloat16 [256, 768], replicated, may hold values from -0.375 to 0.375
- w_hidden: bfloat16 [256, 768], replicated, may hold values from -0.375 to 0.375
- bias_input: float32 [768], replicated, may hold values from -3 to 3
- bias_hidden: float32 [768], replicated, may hold values from -3 to 3
Outputs:
- new_memory: bfloat16 [524288, 256], P(('dom', 'row'))
The draws below stay inside these ranges and needn't reach their ends.
Inputs may be any that keep to these rules, and one draw needn't show every extreme that they name: `target`: -1 marks a padded event row. `source`: values under 65536 name the event's own group, the rest the owner group of the batch; in each batch, of the events of one device at most 24 have a value v < 65536 with v // 2048 equal to one given r, and at most 8 have v >= 65536 with (v - 65536) // 2048 equal to one given r; on every device and batch some r reaches 24 and some r reaches 8.
All inputs are finite; a program needn't handle non-finite values.
Results may differ from the reference program's by a relative error of at most 0.0034.
Values may be sent and summed in bfloat16 or wider, within the bound.
No kernel may reach another device: no remote copies, remote signals or barrier semaphores. Data moves between devices by JAX's collectives and lax.ppermute only.
A program may use at most 64 MiB of HBM per device.

```python
import math
import jax
import jax.numpy as jnp
from jax import lax

W = 256
MSG = 256
TD = 128
EF = 128
B = 4
NODE_DEV = 2048
EV_DEV = 512
NODES = 524288
EVENTS = 131072
N_DOM = 8
N_ROW = 32


def draw_source(key, part):
    cap = 3 * EV_DEV // (2 * N_ROW)
    ocap = EV_DEV // (2 * N_ROW)
    per = cap + ocap
    slots = N_ROW * per
    blocks = B * N_DOM * N_ROW
    first_key, own_key, far_key, node_key = jax.random.split(jax.random.fold_in(key, 17), 4)
    scores = jax.random.randint(first_key, (blocks, slots), 0, 1 << 20)
    full_own = jax.random.randint(own_key, (blocks, 1), 0, N_ROW)
    full_far = jax.random.randint(far_key, (blocks, 1), 0, N_ROW)
    slot_ids = jnp.arange(slots, dtype=jnp.int32)[None, :]
    bucket = slot_ids // per
    is_far = slot_ids % per >= cap
    forced = (bucket == full_own) & jnp.logical_not(is_far) | (bucket == full_far) & is_far
    scores = jnp.where(forced, -1, scores)
    order = jnp.argsort(scores, axis=1, stable=True)[:, :EV_DEV].astype(jnp.int32)
    chosen_bucket = order // per
    chosen_far = order % per >= cap
    node = jax.random.randint(node_key, (blocks, EV_DEV), 0, NODE_DEV)
    local = chosen_bucket * NODE_DEV + node
    value = jnp.where(chosen_far, local + N_ROW * NODE_DEV, local)
    return value.reshape(B, N_DOM * N_ROW * EV_DEV).astype(jnp.int32)


def plant(result, rng, low, high):
    extent = result.shape
    spot = [jax.random.randint(jax.random.fold_in(rng, axis), (), 0, extent[axis]) for axis in range(len(extent))]
    result = result.at[tuple(spot)].set(low)
    longest = extent.index(max(extent))
    spot[longest] = (spot[longest] + 1) % extent[longest]
    return result.at[tuple(spot)].set(high)


def steps_of(key, shape, cuts, smallest, high):
    factor_of = 1.0
    for position, blocks in cuts:
        heights = jax.random.uniform(jax.random.fold_in(jax.random.fold_in(key, 6), position), (blocks,), jnp.float32, smallest / len(cuts), high / len(cuts))
        factor_of = factor_of * jnp.repeat(jnp.exp(heights), shape[position] // blocks).reshape((-1,) + (1,) * (len(shape) - 1 - position))
    return factor_of


def normal_values(key, shape, spread, bound, cuts=(), held_as=jnp.bfloat16):
    entries = spread * jax.random.normal(key, shape, jnp.float32)
    if cuts:
        entries = entries * steps_of(key, shape, cuts, -0.22, 0.18)
    return jnp.clip(entries, -bound, bound).astype(held_as)


def setup_inputs(seed: int = 0) -> dict:
    key_list = jax.random.split(jax.random.key(seed), 15)
    memory = normal_values(key_list[0], (NODES, W), 1.0, 5.0, ((0, 256),))
    node_time = plant(jax.random.randint(key_list[1], (NODES,), 0, 1000), jax.random.fold_in(key_list[1], 1), 0, 999).astype(jnp.int32)
    target = plant(jax.random.randint(key_list[2], (B, EVENTS), -1, NODE_DEV), jax.random.fold_in(key_list[2], 1), -1, NODE_DEV - 1).astype(jnp.int32)
    source = draw_source(jax.random.fold_in(key_list[14], 71), 0)
    event_time = plant(jax.random.randint(key_list[4], (B, EVENTS), 1000, 3000), jax.random.fold_in(key_list[4], 1), 1000, 2999).astype(jnp.int32)
    edge_feat = normal_values(key_list[5], (B, EVENTS, EF), 1.0, 5.0, ((1, 256),))
    owner_group = plant(jax.random.randint(key_list[6], (B,), 0, N_DOM), jax.random.fold_in(key_list[6], 1), 0, N_DOM - 1).astype(jnp.int32)
    w_message = normal_values(key_list[7], (2 * W + TD + EF, MSG), (2 * W + TD + EF) ** -0.5, 0.21875)
    frequency = jnp.clip(jnp.exp(jax.random.uniform(key_list[8], (TD,), jnp.float32, math.log(0.001), math.log(0.1))), 0.001, 0.1)
    phase_shift = jnp.clip(jax.random.uniform(key_list[9], (TD,), jnp.float32, -3.140625, 3.140625), -3.140625, 3.140625)
    w_input = normal_values(key_list[10], (MSG, 3 * W), MSG ** -0.5, 0.375)
    w_hidden = normal_values(key_list[11], (W, 3 * W), W ** -0.5, 0.375)
    bias_input = normal_values(key_list[12], (3 * W,), 0.5, 3.0, (), jnp.float32)
    bias_hidden = normal_values(key_list[13], (3 * W,), 0.5, 3.0, (), jnp.float32)
    return dict(memory=memory, node_time=node_time, target=target, source=source, event_time=event_time, edge_feat=edge_feat, owner_group=owner_group, w_message=w_message, frequency=frequency, phase_shift=phase_shift, w_input=w_input, w_hidden=w_hidden, bias_input=bias_input, bias_hidden=bias_hidden)


def gru_block(pieces, w_input, w_hidden, bias_input, bias_hidden):
    current, averaged, counts = pieces
    mem_width = current.shape[1]
    input_gates = jnp.dot(averaged, w_input, preferred_element_type=jnp.float32) + bias_input
    hidden_gates = jnp.dot(current, w_hidden, preferred_element_type=jnp.float32) + bias_hidden
    reset_gate = jax.nn.sigmoid(input_gates[:, :mem_width] + hidden_gates[:, :mem_width])
    update_gate = jax.nn.sigmoid(input_gates[:, mem_width:2 * mem_width] + hidden_gates[:, mem_width:2 * mem_width])
    candidate = jnp.tanh(input_gates[:, 2 * mem_width:] + reset_gate * hidden_gates[:, 2 * mem_width:])
    previous = current.astype(jnp.float32)
    fresh = (1.0 - update_gate) * candidate + update_gate * previous
    return jnp.where(counts[:, None] > 0, fresh, previous).astype(jnp.bfloat16)


def reference(memory, node_time, target, source, event_time, edge_feat, owner_group, w_message, frequency, phase_shift, w_input, w_hidden, bias_input, bias_hidden):
    mem_width = memory.shape[1]
    time_width = frequency.shape[0]
    group_nodes = N_ROW * NODE_DEV
    node_count = memory.shape[0]
    device_count = node_count // NODE_DEV
    device_of = jnp.arange(target.shape[1], dtype=jnp.int32) // EV_DEV
    group_of = device_of // N_ROW
    current = memory
    times = node_time
    for batch_index in range(B):
        target_now = target[batch_index]
        source_now = source[batch_index]
        valid = target_now >= 0
        target_node = jnp.where(valid, device_of * NODE_DEV + target_now, node_count).astype(jnp.int32)
        source_node = jnp.where(source_now < group_nodes, group_of * group_nodes + source_now,
                                owner_group[batch_index] * group_nodes + source_now - group_nodes).astype(jnp.int32)
        padded_mem = jnp.concatenate([current, jnp.zeros((1, mem_width), jnp.bfloat16)], axis=0)
        padded_time = jnp.concatenate([times, jnp.zeros((1,), jnp.int32)], axis=0)
        mem_target = padded_mem[target_node]
        mem_source = current[source_node]
        last_seen = padded_time[target_node]
        elapsed = (event_time[batch_index] - last_seen).astype(jnp.float32)
        encoded = jnp.cos(elapsed[:, None] * frequency[None, :] + phase_shift[None, :]).astype(jnp.bfloat16)
        base = 2 * mem_width
        message = (jnp.dot(mem_target, w_message[:mem_width], preferred_element_type=jnp.float32)
                   + jnp.dot(mem_source, w_message[mem_width:base], preferred_element_type=jnp.float32)
                   + jnp.dot(encoded, w_message[base:base + time_width], preferred_element_type=jnp.float32)
                   + jnp.dot(edge_feat[batch_index], w_message[base + time_width:], preferred_element_type=jnp.float32)).astype(jnp.bfloat16)
        summed = jax.ops.segment_sum(message.astype(jnp.float32), target_node, node_count + 1)[:node_count]
        counts = jax.ops.segment_sum(valid.astype(jnp.float32), target_node, node_count + 1)[:node_count]
        averaged = (summed / jnp.maximum(counts, 1.0)[:, None]).astype(jnp.bfloat16)
        pieces = (current.reshape(device_count, NODE_DEV, mem_width),
                  averaged.reshape(device_count, NODE_DEV, mem_width),
                  counts.reshape(device_count, NODE_DEV))
        updated = lax.map(lambda piece: gru_block(piece, w_input, w_hidden, bias_input, bias_hidden), pieces)
        current = updated.reshape(node_count, mem_width)
        latest = jax.ops.segment_max(jnp.where(valid, event_time[batch_index], 0).astype(jnp.int32), target_node, node_count + 1)[:node_count]
        times = jnp.maximum(times, latest).astype(jnp.int32)
    return current
```

```python
import functools

import jax
import jax.numpy as jnp
from jax import lax
from jax.experimental import pallas as pl
from jax.experimental.pallas import tpu as pltpu
from jax.sharding import PartitionSpec as P

LANES = 128
F32 = jnp.float32
BF16 = jnp.bfloat16
I32 = jnp.int32
VMEM_LIMIT = 56 * 1024 * 1024


def whole():
    return pl.BlockSpec(memory_space=pltpu.VMEM)


def call(kernel, out_shape, args, flops=0, name=None):
    moved = sum(a.size * a.dtype.itemsize for a in args)
    moved += sum(o.size * o.dtype.itemsize for o in jax.tree.leaves(out_shape))
    return pl.pallas_call(
        kernel,
        out_shape=out_shape,
        in_specs=[whole() for _ in args],
        out_specs=jax.tree.map(lambda _: whole(), out_shape),
        compiler_params=pltpu.CompilerParams(vmem_limit_bytes=VMEM_LIMIT),
        cost_estimate=pl.CostEstimate(flops=flops, bytes_accessed=moved, transcendentals=0),
        name=name,
    )(*args)


def dot(a, b):
    return jnp.dot(a, b, preferred_element_type=F32)


def dot_nt(a, b):
    return lax.dot_general(a, b, (((1,), (1,)), ((), ())), preferred_element_type=F32)


def lane_code(index_col, rows):
    lane = lax.broadcasted_iota(I32, (rows, LANES), 1)
    hit = (index_col & (LANES - 1)) == lane
    return jnp.where(hit, (index_col >> 7).astype(F32), -1.0).astype(BF16)


def expand(code, first, count):
    one = jnp.ones((), BF16)
    zero = jnp.zeros((), BF16)
    return jnp.concatenate(
        [jnp.where(code == jnp.asarray(k, BF16), one, zero) for k in range(first, first + count)],
        axis=1,
    )


def plan_kernel(cap, ocap, node_dev, source_ref, ids_ref, pcode_ref):
    batches, events = source_ref.shape
    rows = ids_ref.shape[0]
    per = cap + ocap
    group_nodes = rows * node_dev
    upper = (
        lax.broadcasted_iota(I32, (events, events), 0)
        <= lax.broadcasted_iota(I32, (events, events), 1)
    ).astype(F32).astype(BF16)
    bucket_iota = lax.broadcasted_iota(I32, (2 * rows, events), 0)
    lane_iota = lax.broadcasted_iota(I32, (LANES, events), 0)
    high = jnp.zeros((rows, LANES), F32)
    low = jnp.zeros((rows, LANES), F32)
    places = []
    for b in range(batches):
        src = source_ref[b : b + 1, :]
        far = src >= group_nodes
        local = jnp.where(far, src - group_nodes, src)
        dest = local // node_dev
        offset = local - dest * node_dev
        bucket = jnp.where(far, dest + rows, dest)
        hit = bucket == bucket_iota
        hitf = hit.astype(F32)
        running = dot(hitf.astype(BF16), upper)
        rank = jnp.sum(hitf * running, axis=0, keepdims=True).astype(I32) - 1
        slot = jnp.where(far, rank + cap, rank) + b * per
        both = (hitf[:rows] + hitf[rows:]).astype(BF16)
        spot = (slot == lane_iota).astype(F32)
        high = high + dot_nt(both, (spot * (offset >> 6).astype(F32)).astype(BF16))
        low = low + dot_nt(both, (spot * (offset & 63).astype(F32)).astype(BF16))
        places.append(jnp.where(far, rows * cap + dest * ocap + rank, dest * cap + rank))
    ids_ref[...] = high.astype(I32) * 64 + low.astype(I32)
    stacked = jnp.concatenate(
        [p.astype(F32) for p in places] + [jnp.zeros((LANES - batches, events), F32)], axis=0
    )
    cols = stacked.T
    for b in range(batches):
        pcode_ref[b] = lane_code(cols[:, b : b + 1].astype(I32), events)


def prep_kernel(
    target_ref,
    time_ref,
    node_time_ref,
    edge_ref,
    freq_ref,
    phase_ref,
    w_enc_ref,
    w_edge_ref,
    base_ref,
    gcode_ref,
    scode_ref,
    same_ref,
    count_ref,
):
    batches, events = target_ref.shape
    node_dev = node_time_ref.shape[1]
    stacked = jnp.concatenate(
        [
            target_ref[...].astype(F32),
            time_ref[...].astype(F32),
            jnp.zeros((LANES - 2 * batches, events), F32),
        ],
        axis=0,
    )
    cols = stacked.T
    sub = lax.broadcasted_iota(I32, (events, events), 0)
    lane = lax.broadcasted_iota(I32, (events, events), 1)
    node_lane = lax.broadcasted_iota(I32, (events, node_dev), 1)
    for b in range(batches):
        tcol = cols[:, b : b + 1].astype(I32)
        ecol = cols[:, batches + b : batches + b + 1]
        seen = jnp.max(
            jnp.where(tcol == node_lane, node_time_ref[...].astype(F32), 0.0), axis=1, keepdims=True
        )
        for before in range(b):
            row = target_ref[before : before + 1, :]
            row = jnp.where(row < 0, -2, row)
            seen = jnp.maximum(
                seen,
                jnp.max(
                    jnp.where(tcol == row, time_ref[before : before + 1, :].astype(F32), 0.0),
                    axis=1,
                    keepdims=True,
                ),
            )
        angle = (ecol - seen) * freq_ref[...] + phase_ref[...]
        encoded = jnp.cos(angle).astype(BF16)
        base_ref[b] = dot(encoded, w_enc_ref[...]) + dot(edge_ref[b], w_edge_ref[...])
        gcode_ref[b] = lane_code(tcol, events)
        trow = target_ref[b : b + 1, :]
        same = (tcol == trow) & (trow >= 0)
        samef = same.astype(F32)
        same_ref[b] = samef.astype(BF16)
        count_ref[b] = jnp.broadcast_to(
            jnp.maximum(jnp.sum(samef, axis=1, keepdims=True), 1.0), (events, LANES)
        )
        earlier = jnp.max(jnp.where(sub < lane, samef, 0.0), axis=0, keepdims=True)
        first = jnp.where(earlier > 0.0, -1, trow)
        sub128 = lax.broadcasted_iota(I32, (LANES, events), 0)
        scode_ref[b] = jnp.where(
            (first & (LANES - 1)) == sub128, (first >> 7).astype(F32), -1.0
        ).astype(BF16)


def serve_rows(table_ref, code_ref, out_ref, step):
    blocks = table_ref.shape[0] // LANES
    table = table_ref[...]
    for start in range(0, code_ref.shape[0], step):
        picked = dot(expand(code_ref[start : start + step, :], 0, blocks), table)
        out_ref[start : start + step, :] = picked.astype(BF16)


def serve_own_kernel(table_ref, own_code_ref, own_ref):
    serve_rows(table_ref, own_code_ref, own_ref, 256)


def serve_far_kernel(table_ref, far_code_ref, far_ref):
    serve_rows(table_ref, far_code_ref, far_ref, 512)


def local_kernel(table_ref, gcode_ref, base_ref, w_target_ref, mem_ref, out_ref):
    blocks = table_ref.shape[0] // LANES
    mem = dot(expand(gcode_ref[...], 0, blocks), table_ref[...]).astype(BF16)
    mem_ref[...] = mem
    out_ref[...] = base_ref[...] + dot(mem, w_target_ref[...])


def update_kernel(
    serve,
    table_ref,
    own_ref,
    far_ref,
    pcode_ref,
    base_ref,
    mem_ref,
    same_ref,
    count_ref,
    scode_ref,
    w_source_ref,
    w_input_ref,
    w_hidden_ref,
    bias_input_ref,
    bias_hidden_ref,
    *rest,
):
    if serve:
        own_code_ref, far_code_ref, new_ref, own_out_ref, far_out_ref = rest
    else:
        (new_ref,) = rest
    width = table_ref.shape[1]
    own_blocks = own_ref.shape[0] // LANES
    far_blocks = far_ref.shape[0] // LANES
    mem = mem_ref[...]
    hidden = dot(mem, w_hidden_ref[...]) + bias_hidden_ref[...]
    pcode = pcode_ref[...]
    source = dot(expand(pcode, 0, own_blocks), own_ref[...]) + dot(
        expand(pcode, own_blocks, far_blocks), far_ref[...]
    )
    message = (base_ref[...] + dot(source.astype(BF16), w_source_ref[...])).astype(BF16)
    total = dot(same_ref[...], message)
    averaged = (total / count_ref[:, :1]).astype(BF16)
    gates = dot(averaged, w_input_ref[...]) + bias_input_ref[...]
    reset = jax.nn.sigmoid(gates[:, :width] + hidden[:, :width])
    update = jax.nn.sigmoid(gates[:, width : 2 * width] + hidden[:, width : 2 * width])
    candidate = jnp.tanh(gates[:, 2 * width :] + reset * hidden[:, 2 * width :])
    fresh = ((1.0 - update) * candidate + update * mem.astype(F32)).astype(BF16)
    ones = jnp.ones((fresh.shape[0], LANES), BF16)
    placed = jnp.concatenate([fresh, ones], axis=1)
    scode = scode_ref[...]
    one = jnp.ones((), BF16)
    zero = jnp.zeros((), BF16)
    blocks = table_ref.shape[0] // LANES
    group = 4
    for k in range(0, blocks, group):
        spread = jnp.concatenate(
            [jnp.where(scode == jnp.asarray(k + j, BF16), one, zero) for j in range(group)], axis=0
        )
        moved = dot(spread, placed)
        rows = slice(k * LANES, (k + group) * LANES)
        new_ref[rows, :] = jnp.where(
            moved[:, width : width + 1] > 0.0, moved[:, :width], table_ref[rows, :].astype(F32)
        ).astype(BF16)
    if serve:
        serve_rows(new_ref, own_code_ref, own_out_ref, 256)
        serve_rows(new_ref, far_code_ref, far_out_ref, 512)


def code_of(index):
    lane = jnp.arange(LANES, dtype=I32)
    low = index & (LANES - 1)
    return jnp.where(low[..., None] == lane, (index >> 7)[..., None], -1).astype(BF16)


def exchange(own_rows, far_rows, owner, row_count, groups):
    width = own_rows.shape[-1]

    def branch(root):
        def body(own_rows, far_rows):
            own_back = lax.all_to_all(own_rows, "row", 0, 0, tiled=True)
            here = lax.axis_index("dom") == root
            mine = jnp.where(here, far_rows[root], jnp.zeros_like(far_rows[root]))
            for shift in range(1, groups):
                other = (root + shift) % groups
                mine = mine + lax.ppermute(far_rows[other], "dom", [(root, other)])
            far_back = lax.all_to_all(
                mine.reshape(row_count, -1, width), "row", 0, 0, tiled=True
            )
            return own_back, far_back

        return body

    own_back, far_back = lax.switch(owner, [branch(r) for r in range(groups)], own_rows, far_rows)
    return own_back.reshape(-1, width), far_back.reshape(-1, width)


def shards(
    memory,
    node_time,
    target,
    source,
    event_time,
    edge_feat,
    owner_group,
    w_message,
    frequency,
    phase_shift,
    w_input,
    w_hidden,
    bias_input,
    bias_hidden,
):
    node_dev, width = memory.shape
    time_width = frequency.shape[0]
    batches, events = target.shape
    rows = lax.axis_size("row")
    groups = lax.axis_size("dom")
    cap = 3 * events // (2 * rows)
    ocap = events // (2 * rows)
    per = cap + ocap
    base_at = 2 * width
    w_target = w_message[:width]
    w_source = w_message[width:base_at]
    w_enc = w_message[base_at : base_at + time_width]
    w_edge = w_message[base_at + time_width :]
    shape = jax.ShapeDtypeStruct

    ids, pcode = call(
        functools.partial(plan_kernel, cap, ocap, node_dev),
        (shape((rows, batches * per), I32), shape((batches, events, LANES), BF16)),
        (source,),
        name="plan",
    )
    got = lax.all_to_all(ids, "row", 0, 0, tiled=True)
    got = got.reshape(rows, batches, per)
    far_ids = got[:, :, cap:].reshape(1, -1)
    asked = lax.all_to_all(
        jnp.broadcast_to(far_ids, (groups, far_ids.shape[1])), "dom", 0, 0, tiled=True
    )
    asked = asked.reshape(groups, rows, batches, ocap)
    own_code = code_of(jnp.transpose(got[:, :, :cap], (1, 0, 2)).reshape(batches, rows * cap))
    far_code = code_of(
        jnp.transpose(asked, (2, 0, 1, 3)).reshape(batches, groups * rows * ocap)
    )
    base, gcode, scode, same, count = call(
        prep_kernel,
        (
            shape((batches, events, width), F32),
            shape((batches, events, LANES), BF16),
            shape((batches, LANES, events), BF16),
            shape((batches, events, events), BF16),
            shape((batches, events, LANES), F32),
        ),
        (
            target,
            event_time,
            node_time.reshape(1, node_dev),
            edge_feat,
            frequency.reshape(1, -1),
            phase_shift.reshape(1, -1),
            w_enc,
            w_edge,
        ),
        name="prep",
    )
    table = memory
    own_rows = call(
        serve_own_kernel, shape((rows * cap, width), BF16), (table, own_code[0]), name="serve_own"
    )
    far_rows = call(
        serve_far_kernel,
        shape((groups * rows * ocap, width), BF16),
        (table, far_code[0]),
        name="serve_far",
    )
    for b in range(batches):
        own_back, far_back = exchange(
            own_rows.reshape(rows, cap, width),
            far_rows.reshape(groups, rows * ocap, width),
            owner_group[b],
            rows,
            groups,
        )
        mem, local = call(
            local_kernel,
            (shape((events, width), BF16), shape((events, width), F32)),
            (table, gcode[b], base[b], w_target),
            name="local",
        )
        serve = b + 1 < batches
        outs = [shape((node_dev, width), BF16)]
        more = ()
        if serve:
            outs += [shape((rows * cap, width), BF16), shape((groups * rows * ocap, width), BF16)]
            more = (own_code[b + 1], far_code[b + 1])
        result = call(
            functools.partial(update_kernel, serve),
            tuple(outs),
            (
                table,
                own_back,
                far_back,
                pcode[b],
                local,
                mem,
                same[b],
                count[b],
                scode[b],
                w_source,
                w_input,
                w_hidden,
                bias_input.reshape(1, -1),
                bias_hidden.reshape(1, -1),
            )
            + more,
            name="update",
        )
        if serve:
            table, own_rows, far_rows = result
        else:
            (table,) = result
    return table


def solution(mesh):
    in_specs = (
        P(("dom", "row"), None),
        P(("dom", "row")),
        P(None, ("dom", "row")),
        P(None, ("dom", "row")),
        P(None, ("dom", "row")),
        P(None, ("dom", "row"), None),
        P(),
        P(),
        P(),
        P(),
        P(),
        P(),
        P(),
        P(),
    )
    out_specs = P(("dom", "row"), None)
    return jax.shard_map(shards, mesh=mesh, in_specs=in_specs, out_specs=out_specs, check_vma=False)
```

```python
import functools

import jax
import jax.numpy as jnp
from jax import lax
from jax.experimental import pallas as pl
from jax.experimental.pallas import tpu as pltpu
from jax.sharding import PartitionSpec as P

LANES = 128
F32 = jnp.float32
BF16 = jnp.bfloat16
I32 = jnp.int32
VMEM_LIMIT = 56 * 1024 * 1024


def whole():
    return pl.BlockSpec(memory_space=pltpu.VMEM)


def call(kernel, out_shape, args, flops=0, name=None, specs=None):
    moved = sum(a.size * a.dtype.itemsize for a in args)
    moved += sum(o.size * o.dtype.itemsize for o in jax.tree.leaves(out_shape))
    specs = specs or {}
    return pl.pallas_call(
        kernel,
        out_shape=out_shape,
        grid=(1,) if specs else (),
        in_specs=[specs.get(i, whole()) for i in range(len(args))],
        out_specs=jax.tree.map(lambda _: whole(), out_shape),
        compiler_params=pltpu.CompilerParams(vmem_limit_bytes=VMEM_LIMIT),
        cost_estimate=pl.CostEstimate(flops=flops, bytes_accessed=moved, transcendentals=0),
        name=name,
    )(*args)


def dot(a, b):
    return jnp.dot(a, b, preferred_element_type=F32)


def dot_nt(a, b):
    return lax.dot_general(a, b, (((1,), (1,)), ((), ())), preferred_element_type=F32)


def lane_code_f32(index_col, rows):
    lane = lax.broadcasted_iota(I32, (rows, LANES), 1)
    hit = (index_col & (LANES - 1)) == lane
    return jnp.where(hit, (index_col >> 7).astype(F32), -1.0)


def lane_code(index_col, rows):
    return lane_code_f32(index_col, rows).astype(BF16)


def expand(code, first, count):
    one = jnp.ones((), BF16)
    zero = jnp.zeros((), BF16)
    return jnp.concatenate(
        [jnp.where(code == jnp.asarray(k, BF16), one, zero) for k in range(first, first + count)],
        axis=1,
    )


def plan_kernel(cap, ocap, node_dev, source_ref, ids_ref, *pcode_refs):
    batches, events = source_ref.shape
    rows = ids_ref.shape[0]
    per = cap + ocap
    group_nodes = rows * node_dev
    upper = (
        lax.broadcasted_iota(I32, (events, events), 0)
        <= lax.broadcasted_iota(I32, (events, events), 1)
    ).astype(F32).astype(BF16)
    bucket_iota = lax.broadcasted_iota(I32, (2 * rows, events), 0)
    lane_iota = lax.broadcasted_iota(I32, (LANES, events), 0)
    high = jnp.zeros((rows, LANES), F32)
    low = jnp.zeros((rows, LANES), F32)
    places = []
    for b in range(batches):
        src = source_ref[b : b + 1, :]
        far = src >= group_nodes
        local = jnp.where(far, src - group_nodes, src)
        dest = local // node_dev
        offset = local - dest * node_dev
        bucket = jnp.where(far, dest + rows, dest)
        hit = bucket == bucket_iota
        hitf = hit.astype(F32)
        running = dot(hitf.astype(BF16), upper)
        rank = jnp.sum(hitf * running, axis=0, keepdims=True).astype(I32) - 1
        slot = jnp.where(far, rank + cap, rank)
        both = (hitf[:rows] + hitf[rows:]).astype(BF16)
        spot = (slot + b * per == lane_iota).astype(F32)
        high = high + dot_nt(both, (spot * (offset >> 6).astype(F32)).astype(BF16))
        low = low + dot_nt(both, (spot * (offset & 63).astype(F32)).astype(BF16))
        places.append(dest * per + slot)
    ids_ref[...] = high.astype(I32) * 64 + low.astype(I32)
    stacked = jnp.concatenate(
        [p.astype(F32) for p in places] + [jnp.zeros((LANES - batches, events), F32)], axis=0
    )
    cols = stacked.T
    for b in range(batches):
        pcode_refs[b][...] = lane_code(cols[:, b : b + 1].astype(I32), events)


def own_code_kernel(b, cap, per, got_ref, code_ref):
    rows, lanes = got_ref.shape
    got = jnp.concatenate([got_ref[...], jnp.zeros((lanes - rows, lanes), I32)], axis=0)
    turned = got.astype(F32).T
    keep = lax.broadcasted_iota(I32, (per, LANES), 0) < cap
    for r in range(rows):
        column = turned[b * per : (b + 1) * per, r : r + 1].astype(I32)
        code = lane_code_f32(column, per)
        code_ref[r * per : (r + 1) * per, :] = jnp.where(keep, code, -1.0).astype(BF16)


def far_code_kernel(b, cap, per, asked_ref, code_ref):
    groups, rows, lanes = asked_ref.shape
    ocap = per - cap
    fill = jnp.zeros((lanes - rows, lanes), I32)
    for g in range(groups):
        turned = jnp.concatenate([asked_ref[g], fill], axis=0).astype(F32).T
        part = turned[b * per + cap : (b + 1) * per, :].astype(I32)
        for r in range(0, rows, 2):
            column = jnp.concatenate([part[:, r : r + 1], part[:, r + 1 : r + 2]], axis=0)
            at = (g * rows + r) * ocap
            code_ref[at : at + 2 * ocap, :] = lane_code(column, 2 * ocap)


def prep_kernel(
    b,
    width,
    target_ref,
    time_ref,
    node_time_ref,
    edge_ref,
    freq_ref,
    phase_ref,
    w_ref,
    base_ref,
    gcode_ref,
    scode_ref,
    same_ref,
    count_ref,
):
    batches, events = target_ref.shape
    node_dev = node_time_ref.shape[1]
    enc_at = 2 * width
    edge_at = enc_at + freq_ref.shape[1]
    stacked = jnp.concatenate(
        [
            target_ref[...].astype(F32),
            time_ref[...].astype(F32),
            jnp.zeros((LANES - 2 * batches, events), F32),
        ],
        axis=0,
    )
    cols = stacked.T
    sub = lax.broadcasted_iota(I32, (events, events), 0)
    lane = lax.broadcasted_iota(I32, (events, events), 1)
    node_lane = lax.broadcasted_iota(I32, (events, node_dev), 1)
    tcol = cols[:, b : b + 1].astype(I32)
    ecol = cols[:, batches + b : batches + b + 1]
    seen = jnp.max(
        jnp.where(tcol == node_lane, node_time_ref[...].astype(F32), 0.0), axis=1, keepdims=True
    )
    for before in range(b):
        row = target_ref[before : before + 1, :]
        row = jnp.where(row < 0, -2, row)
        seen = jnp.maximum(
            seen,
            jnp.max(
                jnp.where(tcol == row, time_ref[before : before + 1, :].astype(F32), 0.0),
                axis=1,
                keepdims=True,
            ),
        )
    angle = (ecol - seen) * freq_ref[...] + phase_ref[...]
    encoded = jnp.cos(angle).astype(BF16)
    base_ref[...] = dot(encoded, w_ref[enc_at:edge_at, :]) + dot(edge_ref[0], w_ref[edge_at:, :])
    gcode_ref[...] = lane_code(tcol, events)
    trow = target_ref[b : b + 1, :]
    same = (tcol == trow) & (trow >= 0)
    samef = same.astype(F32)
    same_ref[...] = samef.astype(BF16)
    count_ref[...] = jnp.broadcast_to(
        jnp.maximum(jnp.sum(samef, axis=1, keepdims=True), 1.0), (events, LANES)
    )
    earlier = jnp.max(jnp.where(sub < lane, samef, 0.0), axis=0, keepdims=True)
    first = jnp.where(earlier > 0.0, -1, trow)
    sub128 = lax.broadcasted_iota(I32, (LANES, events), 0)
    scode_ref[...] = jnp.where(
        (first & (LANES - 1)) == sub128, (first >> 7).astype(F32), -1.0
    ).astype(BF16)


def serve_rows(table_ref, code_ref, out_ref, step):
    blocks = table_ref.shape[0] // LANES
    table = table_ref[...]
    for start in range(0, code_ref.shape[0], step):
        picked = dot(expand(code_ref[start : start + step, :], 0, blocks), table)
        out_ref[start : start + step, :] = picked.astype(BF16)


def serve_own_kernel(table_ref, own_code_ref, own_ref):
    serve_rows(table_ref, own_code_ref, own_ref, 256)


def serve_far_kernel(table_ref, far_code_ref, far_ref):
    serve_rows(table_ref, far_code_ref, far_ref, 512)


def local_kernel(table_ref, gcode_ref, base_ref, w_ref, mem_ref, out_ref):
    blocks = table_ref.shape[0] // LANES
    mem = dot(expand(gcode_ref[...], 0, blocks), table_ref[...]).astype(BF16)
    mem_ref[...] = mem
    out_ref[...] = base_ref[...] + dot(mem, w_ref[: mem.shape[1], :])


def update_kernel(
    serve,
    table_ref,
    back_ref,
    pcode_ref,
    base_ref,
    mem_ref,
    same_ref,
    count_ref,
    scode_ref,
    w_ref,
    w_input_ref,
    w_hidden_ref,
    bias_input_ref,
    bias_hidden_ref,
    *rest,
):
    if serve:
        own_code_ref, far_code_ref, new_ref, own_out_ref, far_out_ref = rest
    else:
        (new_ref,) = rest
    width = table_ref.shape[1]
    mem = mem_ref[...]
    hidden = dot(mem, w_hidden_ref[...]) + bias_hidden_ref[...]
    source = dot(expand(pcode_ref[...], 0, back_ref.shape[0] // LANES), back_ref[...])
    w_source = w_ref[width : 2 * width, :]
    message = (base_ref[...] + dot(source.astype(BF16), w_source)).astype(BF16)
    total = dot(same_ref[...], message)
    averaged = (total / count_ref[:, :1]).astype(BF16)
    gates = dot(averaged, w_input_ref[...]) + bias_input_ref[...]
    reset = jax.nn.sigmoid(gates[:, :width] + hidden[:, :width])
    update = jax.nn.sigmoid(gates[:, width : 2 * width] + hidden[:, width : 2 * width])
    candidate = jnp.tanh(gates[:, 2 * width :] + reset * hidden[:, 2 * width :])
    fresh = ((1.0 - update) * candidate + update * mem.astype(F32)).astype(BF16)
    ones = jnp.ones((fresh.shape[0], LANES), BF16)
    placed = jnp.concatenate([fresh, ones], axis=1)
    scode = scode_ref[...]
    one = jnp.ones((), BF16)
    zero = jnp.zeros((), BF16)
    blocks = table_ref.shape[0] // LANES
    group = 4
    for k in range(0, blocks, group):
        spread = jnp.concatenate(
            [jnp.where(scode == jnp.asarray(k + j, BF16), one, zero) for j in range(group)], axis=0
        )
        moved = dot(spread, placed)
        rows = slice(k * LANES, (k + group) * LANES)
        new_ref[rows, :] = jnp.where(
            moved[:, width : width + 1] > 0.0, moved[:, :width], table_ref[rows, :].astype(F32)
        ).astype(BF16)
    if serve:
        serve_rows(new_ref, own_code_ref, own_out_ref, 256)
        serve_rows(new_ref, far_code_ref, far_out_ref, 512)


def from_owner(own_rows, far_rows, owner, cap):
    rows, _, width = own_rows.shape
    groups = far_rows.shape[0]

    def branch(root):
        def body(own_rows, far_rows):
            me = lax.axis_index("dom")
            mine = far_rows[root]
            for shift in range(1, groups):
                other = (root + shift) % groups
                pairs = [(root, other)]
                if other != root ^ 1:
                    pairs.append((root ^ 1, other ^ 1))
                part = lax.ppermute(far_rows[other], "dom", sorted(pairs))
                mine = jnp.where(me == other, part, mine)
            return own_rows.at[:, cap:, :].set(mine.reshape(rows, -1, width))

        return body

    return lax.switch(owner, [branch(r) for r in range(groups)], own_rows, far_rows)


def shards(
    memory,
    node_time,
    target,
    source,
    event_time,
    edge_feat,
    owner_group,
    w_message,
    frequency,
    phase_shift,
    w_input,
    w_hidden,
    bias_input,
    bias_hidden,
):
    node_dev, width = memory.shape
    batches, events = target.shape
    rows = lax.axis_size("row")
    groups = lax.axis_size("dom")
    cap = 3 * events // (2 * rows)
    ocap = events // (2 * rows)
    per = cap + ocap
    shape = jax.ShapeDtypeStruct
    code = shape((events, LANES), BF16)

    ids, *pcode = call(
        functools.partial(plan_kernel, cap, ocap, node_dev),
        (shape((rows, batches * per), I32),) + (code,) * batches,
        (source,),
        name="plan",
    )
    got = lax.all_to_all(ids, "row", 0, 0, tiled=True)
    asked = lax.all_to_all(
        jnp.broadcast_to(got[None], (groups,) + got.shape), "dom", 0, 0, tiled=True
    )
    times_row = node_time.reshape(1, node_dev)
    freq_row = frequency.reshape(1, -1)
    phase_row = phase_shift.reshape(1, -1)
    input_row = bias_input.reshape(1, -1)
    hidden_row = bias_hidden.reshape(1, -1)

    def own_code(b):
        return call(
            functools.partial(own_code_kernel, b, cap, per),
            shape((rows * per, LANES), BF16),
            (got,),
            flops=10**9,
            name="own_code",
        )

    def far_code(b):
        return call(
            functools.partial(far_code_kernel, b, cap, per),
            shape((groups * rows * ocap, LANES), BF16),
            (asked,),
            flops=2 * 10**9,
            name="far_code",
        )

    def prep(b):
        return call(
            functools.partial(prep_kernel, b, width),
            (
                shape((events, width), F32),
                code,
                shape((LANES, events), BF16),
                shape((events, events), BF16),
                shape((events, LANES), F32),
            ),
            (target, event_time, times_row, edge_feat, freq_row, phase_row, w_message),
            flops=3 * 10**9,
            name="prep",
            specs={3: pl.BlockSpec((1,) + edge_feat.shape[1:], lambda i: (b, 0, 0))},
        )

    table = memory
    own_shape = shape((rows * per, width), BF16)
    far_shape = shape((groups * rows * ocap, width), BF16)
    own_rows = call(
        serve_own_kernel, own_shape, (table, own_code(0)), flops=2 * 10**9, name="serve_own"
    )
    far_rows = call(
        serve_far_kernel, far_shape, (table, far_code(0)), flops=3 * 10**9, name="serve_far"
    )
    for b in range(batches):
        base, gcode, scode, same, count = prep(b)
        sent = from_owner(
            own_rows.reshape(rows, per, width),
            far_rows.reshape(groups, rows * ocap, width),
            owner_group[b],
            cap,
        )
        back = lax.all_to_all(sent, "row", 0, 0, tiled=True).reshape(rows * per, width)
        mem, local = call(
            local_kernel,
            (shape((events, width), BF16), shape((events, width), F32)),
            (table, gcode, base, w_message),
            flops=3 * 10**9,
            name="local",
        )
        serve = b + 1 < batches
        outs = [shape((node_dev, width), BF16)]
        more = ()
        if serve:
            outs += [own_shape, far_shape]
            more = (own_code(b + 1), far_code(b + 1))
        result = call(
            functools.partial(update_kernel, serve),
            tuple(outs),
            (
                table,
                back,
                pcode[b],
                local,
                mem,
                same,
                count,
                scode,
                w_message,
                w_input,
                w_hidden,
                input_row,
                hidden_row,
            )
            + more,
            flops=6 * 10**9,
            name="update",
        )
        if serve:
            table, own_rows, far_rows = result
        else:
            (table,) = result
    return table


def solution(mesh):
    in_specs = (
        P(("dom", "row"), None),
        P(("dom", "row")),
        P(None, ("dom", "row")),
        P(None, ("dom", "row")),
        P(None, ("dom", "row")),
        P(None, ("dom", "row"), None),
        P(),
        P(),
        P(),
        P(),
        P(),
        P(),
        P(),
        P(),
    )
    out_specs = P(("dom", "row"), None)
    return jax.shard_map(shards, mesh=mesh, in_specs=in_specs, out_specs=out_specs, check_vma=False)
```

```python
import functools

import jax
import jax.numpy as jnp
from jax import lax
from jax.experimental import pallas as pl
from jax.experimental.pallas import tpu as pltpu
from jax.sharding import PartitionSpec as P

LANES = 128
F32 = jnp.float32
BF16 = jnp.bfloat16
I32 = jnp.int32
VMEM_LIMIT = 56 * 1024 * 1024


def whole():
    return pl.BlockSpec(memory_space=pltpu.VMEM)


def call(kernel, out_shape, args, flops=0, name=None, specs=None):
    moved = sum(a.size * a.dtype.itemsize for a in args)
    moved += sum(o.size * o.dtype.itemsize for o in jax.tree.leaves(out_shape))
    specs = specs or {}
    return pl.pallas_call(
        kernel,
        out_shape=out_shape,
        grid=(1,) if name == "prep" else (),
        in_specs=[specs.get(i, whole()) for i in range(len(args))],
        out_specs=jax.tree.map(lambda _: whole(), out_shape),
        compiler_params=pltpu.CompilerParams(vmem_limit_bytes=VMEM_LIMIT),
        cost_estimate=pl.CostEstimate(flops=flops, bytes_accessed=moved, transcendentals=0),
        name=name,
    )(*args)


def dot(a, b):
    return jnp.dot(a, b, preferred_element_type=F32)


def dot_nt(a, b):
    return lax.dot_general(a, b, (((1,), (1,)), ((), ())), preferred_element_type=F32)


def lane_code_f32(index_col, rows):
    lane = lax.broadcasted_iota(I32, (rows, LANES), 1)
    hit = (index_col & (LANES - 1)) == lane
    return jnp.where(hit, (index_col >> 7).astype(F32), -1.0)


def lane_code(index_col, rows):
    return lane_code_f32(index_col, rows).astype(BF16)


def expand(code, first, count):
    one = jnp.ones((), BF16)
    zero = jnp.zeros((), BF16)
    return jnp.concatenate(
        [jnp.where(code == jnp.asarray(k, BF16), one, zero) for k in range(first, first + count)],
        axis=1,
    )


def plan_kernel(cap, ocap, node_dev, source_ref, ids_ref, *pcode_refs):
    batches, events = source_ref.shape
    rows = ids_ref.shape[1]
    per = cap + ocap
    group_nodes = rows * node_dev
    upper = (
        lax.broadcasted_iota(I32, (events, events), 0)
        <= lax.broadcasted_iota(I32, (events, events), 1)
    ).astype(F32).astype(BF16)
    bucket_iota = lax.broadcasted_iota(I32, (2 * rows, events), 0)
    lane_iota = lax.broadcasted_iota(I32, (LANES, events), 0)
    high = jnp.zeros((rows, LANES), F32)
    low = jnp.zeros((rows, LANES), F32)
    places = []
    for b in range(batches):
        src = source_ref[b : b + 1, :]
        far = src >= group_nodes
        local = jnp.where(far, src - group_nodes, src)
        dest = local // node_dev
        offset = local - dest * node_dev
        bucket = jnp.where(far, dest + rows, dest)
        hit = bucket == bucket_iota
        hitf = hit.astype(F32)
        running = dot(hitf.astype(BF16), upper)
        rank = jnp.sum(hitf * running, axis=0, keepdims=True).astype(I32) - 1
        slot = jnp.where(far, rank + cap, rank)
        both = (hitf[:rows] + hitf[rows:]).astype(BF16)
        spot = (slot + b * per == lane_iota).astype(F32)
        high = high + dot_nt(both, (spot * (offset >> 6).astype(F32)).astype(BF16))
        low = low + dot_nt(both, (spot * (offset & 63).astype(F32)).astype(BF16))
        places.append(jnp.where(far, rows * cap + dest * ocap + rank, dest * cap + rank))
    ids = high.astype(I32) * 64 + low.astype(I32)
    for g in range(ids_ref.shape[0]):
        ids_ref[g] = ids
    stacked = jnp.concatenate(
        [p.astype(F32) for p in places] + [jnp.zeros((LANES - batches, events), F32)], axis=0
    )
    cols = stacked.T
    for b in range(batches):
        pcode_refs[b][...] = lane_code(cols[:, b : b + 1].astype(I32), events)


def spread_codes(ids, first, count):
    rows = ids.shape[0]
    total = rows * count
    place = lax.broadcasted_iota(I32, (total, LANES), 0)
    lane = lax.broadcasted_iota(I32, (total, LANES), 1)
    row = place // count
    copy = (row[:, :rows] == lane[:, :rows]).astype(F32).astype(BF16)
    keep = (lane == first + place - row * count).astype(F32)
    ones = jnp.ones((LANES, LANES), BF16)

    def everywhere(part):
        taken = dot(copy, part.astype(F32).astype(BF16)) * keep
        return dot(taken.astype(BF16), ones)

    low = everywhere(ids & (LANES - 1))
    high = everywhere(ids >> 7)
    return jnp.where(low == lane.astype(F32), high, -1.0).astype(BF16)


def code_kernel(b, cap, per, me_ref, asked_ref, own_ref, far_ref):
    groups, rows, _ = asked_ref.shape
    own_ref[...] = spread_codes(asked_ref[me_ref[0]], b * per, cap)
    block = rows * (per - cap)
    for g in range(groups):
        far_ref[g * block : (g + 1) * block, :] = spread_codes(
            asked_ref[g], b * per + cap, per - cap
        )


def cosine(x):
    turns = jnp.floor(x * 0.15915494309189535 + 0.5)
    r = (x - turns * 6.28125) - turns * 0.0019353071795864769
    z = r * r
    value = jnp.full_like(z, 1.0 / 20922789888000.0)
    for factor in (
        -1.0 / 87178291200.0,
        1.0 / 479001600.0,
        -1.0 / 3628800.0,
        1.0 / 40320.0,
        -1.0 / 720.0,
        1.0 / 24.0,
        -0.5,
        1.0,
    ):
        value = value * z + factor
    return value


def prep_kernel(
    b,
    width,
    target_ref,
    time_ref,
    node_time_ref,
    edge_ref,
    freq_ref,
    phase_ref,
    w_ref,
    base_ref,
    gcode_ref,
    scode_ref,
    same_ref,
    count_ref,
):
    batches, events = target_ref.shape
    node_dev = node_time_ref.shape[1]
    enc_at = 2 * width
    edge_at = enc_at + freq_ref.shape[1]
    stacked = jnp.concatenate(
        [
            target_ref[...].astype(F32),
            time_ref[...].astype(F32),
            jnp.zeros((LANES - 2 * batches, events), F32),
        ],
        axis=0,
    )
    cols = stacked.T
    sub = lax.broadcasted_iota(I32, (events, events), 0)
    lane = lax.broadcasted_iota(I32, (events, events), 1)
    node_lane = lax.broadcasted_iota(I32, (events, node_dev), 1)
    tcol = cols[:, b : b + 1].astype(I32)
    ecol = cols[:, batches + b : batches + b + 1]
    seen = jnp.max(
        jnp.where(tcol == node_lane, node_time_ref[...].astype(F32), 0.0), axis=1, keepdims=True
    )
    for before in range(b):
        row = target_ref[before : before + 1, :]
        row = jnp.where(row < 0, -2, row)
        seen = jnp.maximum(
            seen,
            jnp.max(
                jnp.where(tcol == row, time_ref[before : before + 1, :].astype(F32), 0.0),
                axis=1,
                keepdims=True,
            ),
        )
    angle = (ecol - seen) * freq_ref[...] + phase_ref[...]
    encoded = cosine(angle).astype(BF16)
    base_ref[...] = dot(encoded, w_ref[enc_at:edge_at, :]) + dot(edge_ref[0], w_ref[edge_at:, :])
    gcode_ref[...] = lane_code(tcol, events)
    trow = target_ref[b : b + 1, :]
    same = (tcol == trow) & (trow >= 0)
    samef = same.astype(F32)
    same_ref[...] = samef.astype(BF16)
    count_ref[...] = jnp.broadcast_to(
        jnp.maximum(jnp.sum(samef, axis=1, keepdims=True), 1.0), (events, LANES)
    )
    earlier = jnp.max(jnp.where(sub < lane, samef, 0.0), axis=0, keepdims=True)
    first = jnp.where(earlier > 0.0, -1, trow)
    sub128 = lax.broadcasted_iota(I32, (LANES, events), 0)
    scode_ref[...] = jnp.where(
        (first & (LANES - 1)) == sub128, (first >> 7).astype(F32), -1.0
    ).astype(BF16)


def serve_rows(table_ref, code_ref, out_ref, step):
    blocks = table_ref.shape[0] // LANES
    table = table_ref[...]
    for start in range(0, code_ref.shape[0], step):
        picked = dot(expand(code_ref[start : start + step, :], 0, blocks), table)
        out_ref[start : start + step, :] = picked.astype(BF16)


def serve_kernel(table_ref, own_code_ref, far_code_ref, own_ref, far_ref):
    serve_rows(table_ref, own_code_ref, own_ref, 256)
    serve_rows(table_ref, far_code_ref, far_ref, 512)


def local_kernel(table_ref, gcode_ref, base_ref, w_ref, mem_ref, out_ref):
    blocks = table_ref.shape[0] // LANES
    mem = dot(expand(gcode_ref[...], 0, blocks), table_ref[...]).astype(BF16)
    mem_ref[...] = mem
    out_ref[...] = base_ref[...] + dot(mem, w_ref[: mem.shape[1], :])


def update_kernel(
    serve,
    table_ref,
    own_ref,
    far_ref,
    pcode_ref,
    base_ref,
    mem_ref,
    same_ref,
    count_ref,
    scode_ref,
    w_ref,
    w_input_ref,
    w_hidden_ref,
    bias_input_ref,
    bias_hidden_ref,
    *rest,
):
    if serve:
        own_code_ref, far_code_ref, new_ref, own_out_ref, far_out_ref = rest
    else:
        (new_ref,) = rest
    width = table_ref.shape[1]
    mem = mem_ref[...]
    hidden = dot(mem, w_hidden_ref[...]) + bias_hidden_ref[...]
    own_blocks = own_ref.shape[0] // LANES
    far_blocks = far_ref.shape[0] // LANES
    pcode = pcode_ref[...]
    source = dot(expand(pcode, 0, own_blocks), own_ref[...]) + dot(
        expand(pcode, own_blocks, far_blocks), far_ref[...]
    )
    w_source = w_ref[width : 2 * width, :]
    message = (base_ref[...] + dot(source.astype(BF16), w_source)).astype(BF16)
    total = dot(same_ref[...], message)
    averaged = (total / count_ref[:, :1]).astype(BF16)
    gates = dot(averaged, w_input_ref[...]) + bias_input_ref[...]
    reset = jax.nn.sigmoid(gates[:, :width] + hidden[:, :width])
    update = jax.nn.sigmoid(gates[:, width : 2 * width] + hidden[:, width : 2 * width])
    candidate = jnp.tanh(gates[:, 2 * width :] + reset * hidden[:, 2 * width :])
    fresh = ((1.0 - update) * candidate + update * mem.astype(F32)).astype(BF16)
    ones = jnp.ones((fresh.shape[0], LANES), BF16)
    placed = jnp.concatenate([fresh, ones], axis=1)
    scode = scode_ref[...]
    one = jnp.ones((), BF16)
    zero = jnp.zeros((), BF16)
    blocks = table_ref.shape[0] // LANES
    group = 4
    for k in range(0, blocks, group):
        spread = jnp.concatenate(
            [jnp.where(scode == jnp.asarray(k + j, BF16), one, zero) for j in range(group)], axis=0
        )
        moved = dot(spread, placed)
        rows = slice(k * LANES, (k + group) * LANES)
        new_ref[rows, :] = jnp.where(
            moved[:, width : width + 1] > 0.0, moved[:, :width], table_ref[rows, :].astype(F32)
        ).astype(BF16)
    if serve:
        serve_rows(new_ref, own_code_ref, own_out_ref, 256)
        serve_rows(new_ref, far_code_ref, far_out_ref, 512)


def fetch(own_rows, far_rows, owner):
    groups = far_rows.shape[0]

    def branch(pair):
        left, right = 2 * pair, 2 * pair + 1

        def body(own_rows, far_rows):
            me = lax.axis_index("dom")
            parts = []
            for shift in range(1, groups // 2):
                there = (pair + shift) % (groups // 2)
                for flip in range(2):
                    to_left, to_right = 2 * there + flip, 2 * there + 1 - flip
                    rows = jnp.where(me == left, far_rows[to_left], far_rows[to_right])
                    part = lax.ppermute(rows, "dom", [(left, to_left), (right, to_right)])
                    parts.append((to_left, to_right, part))
            rows = jnp.where(me == left, far_rows[right], far_rows[left])
            part = lax.ppermute(rows, "dom", [(left, right), (right, left)])
            parts.append((right, left, part))
            own_back = lax.all_to_all(own_rows, "row", 0, 0, tiled=True)
            seat = me + (own_back[0, 0, 0].astype(F32) * 0.0).astype(I32)
            mine = jnp.where(owner == left, far_rows[left], far_rows[right])
            for to_left, to_right, part in parts:
                wanted = jnp.where(owner == left, to_left, to_right)
                mine = jnp.where(seat == wanted, part, mine)
            return own_back, mine

        return body

    return lax.switch(owner // 2, [branch(p) for p in range(groups // 2)], own_rows, far_rows)


def shards(
    memory,
    node_time,
    target,
    source,
    event_time,
    edge_feat,
    owner_group,
    w_message,
    frequency,
    phase_shift,
    w_input,
    w_hidden,
    bias_input,
    bias_hidden,
):
    node_dev, width = memory.shape
    batches, events = target.shape
    rows = lax.axis_size("row")
    groups = lax.axis_size("dom")
    cap = 3 * events // (2 * rows)
    ocap = events // (2 * rows)
    per = cap + ocap
    shape = jax.ShapeDtypeStruct
    code = shape((events, LANES), BF16)

    ids, *pcode = call(
        functools.partial(plan_kernel, cap, ocap, node_dev),
        (shape((groups, rows, batches * per), I32),) + (code,) * batches,
        (source,),
        name="plan",
    )
    asked = lax.all_to_all(
        ids.reshape(groups * rows, 1, batches * per), ("dom", "row"), 0, 0, tiled=True
    ).reshape(groups, rows, batches * per)
    me = lax.axis_index("dom").astype(I32).reshape(1)
    times_row = node_time.reshape(1, node_dev)
    freq_row = frequency.reshape(1, -1)
    phase_row = phase_shift.reshape(1, -1)
    input_row = bias_input.reshape(1, -1)
    hidden_row = bias_hidden.reshape(1, -1)

    def codes(b):
        return call(
            functools.partial(code_kernel, b, cap, per),
            (
                shape((rows * cap, LANES), BF16),
                shape((groups * rows * ocap, LANES), BF16),
            ),
            (me, asked),
            flops=2 * 10**9,
            name="codes",
            specs={0: pl.BlockSpec(memory_space=pltpu.SMEM)},
        )

    def prep(b):
        return call(
            functools.partial(prep_kernel, b, width),
            (
                shape((events, width), F32),
                code,
                shape((LANES, events), BF16),
                shape((events, events), BF16),
                shape((events, LANES), F32),
            ),
            (target, event_time, times_row, edge_feat, freq_row, phase_row, w_message),
            flops=3 * 10**9,
            name="prep",
            specs={3: pl.BlockSpec((1,) + edge_feat.shape[1:], lambda i: (b, 0, 0))},
        )

    table = memory
    own_shape = shape((rows * cap, width), BF16)
    far_shape = shape((groups * rows * ocap, width), BF16)
    own_rows, far_rows = call(
        serve_kernel, (own_shape, far_shape), (table,) + tuple(codes(0)), flops=4 * 10**9, name="serve"
    )
    for b in range(batches):
        base, gcode, scode, same, count = prep(b)
        own_back, mine = fetch(
            own_rows.reshape(rows, cap, width),
            far_rows.reshape(groups, rows * ocap, width),
            owner_group[b],
        )
        far_back = lax.all_to_all(mine.reshape(rows, ocap, width), "row", 0, 0, tiled=True)
        mem, local = call(
            local_kernel,
            (shape((events, width), BF16), shape((events, width), F32)),
            (table, gcode, base, w_message),
            flops=3 * 10**9,
            name="local",
        )
        serve = b + 1 < batches
        outs = [shape((node_dev, width), BF16)]
        more = ()
        if serve:
            outs += [own_shape, far_shape]
            more = tuple(codes(b + 1))
        result = call(
            functools.partial(update_kernel, serve),
            tuple(outs),
            (
                table,
                own_back.reshape(rows * cap, width),
                far_back.reshape(rows * ocap, width),
                pcode[b],
                local,
                mem,
                same,
                count,
                scode,
                w_message,
                w_input,
                w_hidden,
                input_row,
                hidden_row,
            )
            + more,
            flops=6 * 10**9,
            name="update",
        )
        if serve:
            table, own_rows, far_rows = result
        else:
            (table,) = result
    return table


def solution(mesh):
    in_specs = (
        P(("dom", "row"), None),
        P(("dom", "row")),
        P(None, ("dom", "row")),
        P(None, ("dom", "row")),
        P(None, ("dom", "row")),
        P(None, ("dom", "row"), None),
        P(),
        P(),
        P(),
        P(),
        P(),
        P(),
        P(),
        P(),
    )
    out_specs = P(("dom", "row"), None)
    return jax.shard_map(shards, mesh=mesh, in_specs=in_specs, out_specs=out_specs, check_vma=False)
```

```python
import functools

import jax
import jax.numpy as jnp
from jax import lax
from jax.experimental import pallas as pl
from jax.experimental.pallas import tpu as pltpu
from jax.sharding import PartitionSpec as P

LANES = 128
F32 = jnp.float32
BF16 = jnp.bfloat16
I32 = jnp.int32
VMEM_LIMIT = 56 * 1024 * 1024


def whole():
    return pl.BlockSpec(memory_space=pltpu.VMEM)


def call(kernel, out_shape, args, flops=0, name=None, specs=None):
    moved = sum(a.size * a.dtype.itemsize for a in args)
    moved += sum(o.size * o.dtype.itemsize for o in jax.tree.leaves(out_shape))
    specs = specs or {}
    return pl.pallas_call(
        kernel,
        out_shape=out_shape,
        grid=(1,) if name == "prep" else (),
        in_specs=[specs.get(i, whole()) for i in range(len(args))],
        out_specs=jax.tree.map(lambda _: whole(), out_shape),
        compiler_params=pltpu.CompilerParams(vmem_limit_bytes=VMEM_LIMIT),
        cost_estimate=pl.CostEstimate(flops=flops, bytes_accessed=moved, transcendentals=0),
        name=name,
    )(*args)


def dot(a, b):
    return jnp.dot(a, b, preferred_element_type=F32)


def dot_nt(a, b):
    return lax.dot_general(a, b, (((1,), (1,)), ((), ())), preferred_element_type=F32)


def lane_code_f32(index_col, rows):
    lane = lax.broadcasted_iota(I32, (rows, LANES), 1)
    hit = (index_col & (LANES - 1)) == lane
    return jnp.where(hit, (index_col >> 7).astype(F32), -1.0)


def lane_code(index_col, rows):
    return lane_code_f32(index_col, rows).astype(BF16)


def expand(code, first, count):
    one = jnp.ones((), BF16)
    zero = jnp.zeros((), BF16)
    return jnp.concatenate(
        [jnp.where(code == jnp.asarray(k, BF16), one, zero) for k in range(first, first + count)],
        axis=1,
    )


def plan_kernel(cap, ocap, node_dev, source_ref, ids_ref, *pcode_refs):
    batches, events = source_ref.shape
    rows = ids_ref.shape[1]
    per = cap + ocap
    group_nodes = rows * node_dev
    upper = (
        lax.broadcasted_iota(I32, (events, events), 0)
        <= lax.broadcasted_iota(I32, (events, events), 1)
    ).astype(F32).astype(BF16)
    bucket_iota = lax.broadcasted_iota(I32, (2 * rows, events), 0)
    lane_iota = lax.broadcasted_iota(I32, (LANES, events), 0)
    high = jnp.zeros((rows, LANES), F32)
    low = jnp.zeros((rows, LANES), F32)
    places = []
    for b in range(batches):
        src = source_ref[b : b + 1, :]
        far = src >= group_nodes
        local = jnp.where(far, src - group_nodes, src)
        dest = local // node_dev
        offset = local - dest * node_dev
        bucket = jnp.where(far, dest + rows, dest)
        hit = bucket == bucket_iota
        hitf = hit.astype(F32)
        running = dot(hitf.astype(BF16), upper)
        rank = jnp.sum(hitf * running, axis=0, keepdims=True).astype(I32) - 1
        slot = jnp.where(far, rank + cap, rank)
        both = (hitf[:rows] + hitf[rows:]).astype(BF16)
        spot = (slot + b * per == lane_iota).astype(F32)
        high = high + dot_nt(both, (spot * (offset >> 6).astype(F32)).astype(BF16))
        low = low + dot_nt(both, (spot * (offset & 63).astype(F32)).astype(BF16))
        places.append(dest * per + slot)
    ids = high.astype(I32) * 64 + low.astype(I32)
    for g in range(ids_ref.shape[0]):
        ids_ref[g] = ids
    stacked = jnp.concatenate(
        [p.astype(F32) for p in places] + [jnp.zeros((LANES - batches, events), F32)], axis=0
    )
    cols = stacked.T
    for b in range(batches):
        pcode_refs[b][...] = lane_code(cols[:, b : b + 1].astype(I32), events)


def spread_codes(ids, first, count):
    rows = ids.shape[0]
    total = rows * count
    place = lax.broadcasted_iota(I32, (total, LANES), 0)
    lane = lax.broadcasted_iota(I32, (total, LANES), 1)
    row = place // count
    copy = (row[:, :rows] == lane[:, :rows]).astype(F32).astype(BF16)
    keep = (lane == first + place - row * count).astype(F32)
    ones = jnp.ones((LANES, LANES), BF16)

    def everywhere(part):
        taken = dot(copy, part.astype(F32).astype(BF16)) * keep
        return dot(taken.astype(BF16), ones)

    low = everywhere(ids & (LANES - 1))
    high = everywhere(ids >> 7)
    return jnp.where(low == lane.astype(F32), high, -1.0).astype(BF16)


def code_kernel(b, cap, per, me_ref, asked_ref, _, own_ref, far_ref):
    groups, rows, _ = asked_ref.shape
    own_ref[...] = spread_codes(asked_ref[me_ref[0]], b * per, per)
    block = rows * (per - cap)
    for g in range(groups):
        far_ref[g * block : (g + 1) * block, :] = spread_codes(
            asked_ref[g], b * per + cap, per - cap
        )


def cosine(x):
    turns = jnp.floor(x * 0.15915494309189535 + 0.5)
    r = (x - turns * 6.28125) - turns * 0.0019353071795864769
    z = r * r
    value = jnp.full_like(z, 1.0 / 20922789888000.0)
    for factor in (
        -1.0 / 87178291200.0,
        1.0 / 479001600.0,
        -1.0 / 3628800.0,
        1.0 / 40320.0,
        -1.0 / 720.0,
        1.0 / 24.0,
        -0.5,
        1.0,
    ):
        value = value * z + factor
    return value


def prep_kernel(
    b,
    width,
    target_ref,
    time_ref,
    node_time_ref,
    edge_ref,
    freq_ref,
    phase_ref,
    w_ref,
    _,
    base_ref,
    gcode_ref,
    scode_ref,
    same_ref,
    count_ref,
):
    batches, events = target_ref.shape
    node_dev = node_time_ref.shape[1]
    enc_at = 2 * width
    edge_at = enc_at + freq_ref.shape[1]
    stacked = jnp.concatenate(
        [
            target_ref[...].astype(F32),
            time_ref[...].astype(F32),
            jnp.zeros((LANES - 2 * batches, events), F32),
        ],
        axis=0,
    )
    cols = stacked.T
    sub = lax.broadcasted_iota(I32, (events, events), 0)
    lane = lax.broadcasted_iota(I32, (events, events), 1)
    node_lane = lax.broadcasted_iota(I32, (events, node_dev), 1)
    tcol = cols[:, b : b + 1].astype(I32)
    ecol = cols[:, batches + b : batches + b + 1]
    seen = jnp.max(
        jnp.where(tcol == node_lane, node_time_ref[...].astype(F32), 0.0), axis=1, keepdims=True
    )
    for before in range(b):
        row = target_ref[before : before + 1, :]
        row = jnp.where(row < 0, -2, row)
        seen = jnp.maximum(
            seen,
            jnp.max(
                jnp.where(tcol == row, time_ref[before : before + 1, :].astype(F32), 0.0),
                axis=1,
                keepdims=True,
            ),
        )
    angle = (ecol - seen) * freq_ref[...] + phase_ref[...]
    encoded = cosine(angle).astype(BF16)
    base_ref[...] = dot(encoded, w_ref[enc_at:edge_at, :]) + dot(edge_ref[0], w_ref[edge_at:, :])
    gcode_ref[...] = lane_code(tcol, events)
    trow = target_ref[b : b + 1, :]
    same = (tcol == trow) & (trow >= 0)
    samef = same.astype(F32)
    same_ref[...] = samef.astype(BF16)
    count_ref[...] = jnp.broadcast_to(
        jnp.maximum(jnp.sum(samef, axis=1, keepdims=True), 1.0), (events, LANES)
    )
    earlier = jnp.max(jnp.where(sub < lane, samef, 0.0), axis=0, keepdims=True)
    first = jnp.where(earlier > 0.0, -1, trow)
    sub128 = lax.broadcasted_iota(I32, (LANES, events), 0)
    scode_ref[...] = jnp.where(
        (first & (LANES - 1)) == sub128, (first >> 7).astype(F32), -1.0
    ).astype(BF16)


def serve_rows(table_ref, code_ref, out_ref, step):
    blocks = table_ref.shape[0] // LANES
    table = table_ref[...]
    for start in range(0, code_ref.shape[0], step):
        picked = dot(expand(code_ref[start : start + step, :], 0, blocks), table)
        out_ref[start : start + step, :] = picked.astype(BF16)


def serve_kernel(table_ref, own_code_ref, far_code_ref, own_ref, far_ref):
    serve_rows(table_ref, own_code_ref, own_ref, 256)
    serve_rows(table_ref, far_code_ref, far_ref, 512)


def local_kernel(table_ref, gcode_ref, base_ref, w_ref, mem_ref, out_ref):
    blocks = table_ref.shape[0] // LANES
    mem = dot(expand(gcode_ref[...], 0, blocks), table_ref[...]).astype(BF16)
    mem_ref[...] = mem
    out_ref[...] = base_ref[...] + dot(mem, w_ref[: mem.shape[1], :])


def update_kernel(
    serve,
    table_ref,
    back_ref,
    pcode_ref,
    base_ref,
    mem_ref,
    same_ref,
    count_ref,
    scode_ref,
    w_ref,
    w_input_ref,
    w_hidden_ref,
    bias_input_ref,
    bias_hidden_ref,
    *rest,
):
    if serve:
        own_code_ref, far_code_ref, new_ref, own_out_ref, far_out_ref = rest
    else:
        (new_ref,) = rest
    width = table_ref.shape[1]
    mem = mem_ref[...]
    hidden = dot(mem, w_hidden_ref[...]) + bias_hidden_ref[...]
    source = dot(expand(pcode_ref[...], 0, back_ref.shape[0] // LANES), back_ref[...])
    w_source = w_ref[width : 2 * width, :]
    message = (base_ref[...] + dot(source.astype(BF16), w_source)).astype(BF16)
    total = dot(same_ref[...], message)
    averaged = (total / count_ref[:, :1]).astype(BF16)
    gates = dot(averaged, w_input_ref[...]) + bias_input_ref[...]
    reset = jax.nn.sigmoid(gates[:, :width] + hidden[:, :width])
    update = jax.nn.sigmoid(gates[:, width : 2 * width] + hidden[:, width : 2 * width])
    candidate = jnp.tanh(gates[:, 2 * width :] + reset * hidden[:, 2 * width :])
    fresh = ((1.0 - update) * candidate + update * mem.astype(F32)).astype(BF16)
    ones = jnp.ones((fresh.shape[0], LANES), BF16)
    placed = jnp.concatenate([fresh, ones], axis=1)
    scode = scode_ref[...]
    one = jnp.ones((), BF16)
    zero = jnp.zeros((), BF16)
    blocks = table_ref.shape[0] // LANES
    group = 4
    for k in range(0, blocks, group):
        spread = jnp.concatenate(
            [jnp.where(scode == jnp.asarray(k + j, BF16), one, zero) for j in range(group)], axis=0
        )
        moved = dot(spread, placed)
        rows = slice(k * LANES, (k + group) * LANES)
        new_ref[rows, :] = jnp.where(
            moved[:, width : width + 1] > 0.0, moved[:, :width], table_ref[rows, :].astype(F32)
        ).astype(BF16)
    if serve:
        serve_rows(new_ref, own_code_ref, own_out_ref, 256)
        serve_rows(new_ref, far_code_ref, far_out_ref, 512)


def from_owner(own_rows, far_rows, owner, cap):
    rows, _, width = own_rows.shape
    ys = far_rows.shape[0] // 2

    def branch(y):
        def body(own_rows, far_rows):
            me = lax.axis_index("dom")
            my_y, my_z = me // 2, me % 2
            z = owner % 2

            def spread(which):
                part = lax.dynamic_index_in_dim(far_rows, 2 * y + which, 0, keepdims=False)
                moved = []
                for shift in range(1, ys):
                    there = (y + shift) % ys
                    block = lax.dynamic_index_in_dim(far_rows, 2 * there + which, 0, keepdims=False)
                    pairs = [(2 * y + side, 2 * there + side) for side in range(2)]
                    moved.append((there, lax.ppermute(block, "dom", pairs)))
                for there, block in moved:
                    part = jnp.where(my_y == there, block, part)
                return part

            across = spread(1 - z)
            along = spread(z)
            up = lax.ppermute(across, "dom", [(2 * i, 2 * i + 1) for i in range(ys)])
            down = lax.ppermute(across, "dom", [(2 * i + 1, 2 * i) for i in range(ys)])
            mine = jnp.where(my_z == z, along, jnp.where(z == 0, up, down))
            return own_rows.at[:, cap:, :].set(mine.reshape(rows, -1, width))

        return body

    return lax.switch(owner // 2, [branch(y) for y in range(ys)], own_rows, far_rows)


def shards(
    memory,
    node_time,
    target,
    source,
    event_time,
    edge_feat,
    owner_group,
    w_message,
    frequency,
    phase_shift,
    w_input,
    w_hidden,
    bias_input,
    bias_hidden,
):
    node_dev, width = memory.shape
    batches, events = target.shape
    rows = lax.axis_size("row")
    groups = lax.axis_size("dom")
    cap = 3 * events // (2 * rows)
    ocap = events // (2 * rows)
    per = cap + ocap
    shape = jax.ShapeDtypeStruct
    code = shape((events, LANES), BF16)

    ids, *pcode = call(
        functools.partial(plan_kernel, cap, ocap, node_dev),
        (shape((groups, rows, batches * per), I32),) + (code,) * batches,
        (source,),
        name="plan",
    )
    asked = lax.all_to_all(
        ids.reshape(groups * rows, 1, batches * per), ("dom", "row"), 0, 0, tiled=True
    ).reshape(groups, rows, batches * per)
    me = lax.axis_index("dom").astype(I32).reshape(1)
    times_row = node_time.reshape(1, node_dev)
    freq_row = frequency.reshape(1, -1)
    phase_row = phase_shift.reshape(1, -1)
    input_row = bias_input.reshape(1, -1)
    hidden_row = bias_hidden.reshape(1, -1)

    def codes(b, after):
        return call(
            functools.partial(code_kernel, b, cap, per),
            (
                shape((rows * per, LANES), BF16),
                shape((groups * rows * ocap, LANES), BF16),
            ),
            (me, asked, after),
            flops=2 * 10**9,
            name="codes",
            specs={0: pl.BlockSpec(memory_space=pltpu.SMEM), 2: pl.BlockSpec(memory_space=pl.ANY)},
        )

    def prep(b, after):
        return call(
            functools.partial(prep_kernel, b, width),
            (
                shape((events, width), F32),
                code,
                shape((LANES, events), BF16),
                shape((events, events), BF16),
                shape((events, LANES), F32),
            ),
            (target, event_time, times_row, edge_feat, freq_row, phase_row, w_message, after),
            flops=3 * 10**9,
            name="prep",
            specs={
                3: pl.BlockSpec((1,) + edge_feat.shape[1:], lambda i: (b, 0, 0)),
                7: pl.BlockSpec(memory_space=pl.ANY),
            },
        )

    table = memory
    own_shape = shape((rows * per, width), BF16)
    far_shape = shape((groups * rows * ocap, width), BF16)
    own_rows, far_rows = call(
        serve_kernel, (own_shape, far_shape), (table,) + tuple(codes(0, asked)), flops=4 * 10**9, name="serve"
    )
    ready = prep(0, ids)
    for b in range(batches):
        base, gcode, scode, same, count = ready
        serve = b + 1 < batches
        sent = from_owner(
            own_rows.reshape(rows, per, width),
            far_rows.reshape(groups, rows * ocap, width),
            owner_group[b],
            cap,
        )
        back = lax.all_to_all(sent, "row", 0, 0, tiled=True).reshape(rows * per, width)
        mem, local = call(
            local_kernel,
            (shape((events, width), BF16), shape((events, width), F32)),
            (table, gcode, base, w_message),
            flops=3 * 10**9,
            name="local",
        )
        outs = [shape((node_dev, width), BF16)]
        more = ()
        if serve:
            outs += [own_shape, far_shape]
            more = tuple(codes(b + 1, sent))
            ready = prep(b + 1, sent)
        result = call(
            functools.partial(update_kernel, serve),
            tuple(outs),
            (
                table,
                back,
                pcode[b],
                local,
                mem,
                same,
                count,
                scode,
                w_message,
                w_input,
                w_hidden,
                input_row,
                hidden_row,
            )
            + more,
            flops=6 * 10**9,
            name="update",
        )
        if serve:
            table, own_rows, far_rows = result
        else:
            (table,) = result
    return table


def solution(mesh):
    in_specs = (
        P(("dom", "row"), None),
        P(("dom", "row")),
        P(None, ("dom", "row")),
        P(None, ("dom", "row")),
        P(None, ("dom", "row")),
        P(None, ("dom", "row"), None),
        P(),
        P(),
        P(),
        P(),
        P(),
        P(),
        P(),
        P(),
    )
    out_specs = P(("dom", "row"), None)
    return jax.shard_map(shards, mesh=mesh, in_specs=in_specs, out_specs=out_specs, check_vma=False)
```

```python
import functools

import jax
import jax.numpy as jnp
from jax import lax
from jax.experimental import pallas as pl
from jax.experimental.pallas import tpu as pltpu
from jax.sharding import PartitionSpec as P

LANES = 128
F32 = jnp.float32
BF16 = jnp.bfloat16
I32 = jnp.int32
VMEM_LIMIT = 56 * 1024 * 1024


def whole():
    return pl.BlockSpec(memory_space=pltpu.VMEM)


def call(kernel, out_shape, args, flops=0, name=None, specs=None, scalars=(), aliases=None):
    moved = sum(a.size * a.dtype.itemsize for a in args)
    moved += sum(o.size * o.dtype.itemsize for o in jax.tree.leaves(out_shape))
    specs = specs or {}
    return pl.pallas_call(
        kernel,
        out_shape=out_shape,
        grid_spec=pltpu.PrefetchScalarGridSpec(
            num_scalar_prefetch=len(scalars),
            grid=(1,) if scalars else (),
            in_specs=[specs.get(i, whole()) for i in range(len(args))],
            out_specs=jax.tree.map(lambda _: whole(), out_shape),
        ),
        input_output_aliases=aliases or {},
        compiler_params=pltpu.CompilerParams(vmem_limit_bytes=VMEM_LIMIT),
        cost_estimate=pl.CostEstimate(flops=flops, bytes_accessed=moved, transcendentals=0),
        name=name,
    )(*scalars, *args)


def dot(a, b):
    return jnp.dot(a, b, preferred_element_type=F32)


def dot_nt(a, b):
    return lax.dot_general(a, b, (((1,), (1,)), ((), ())), preferred_element_type=F32)


def lane_code_f32(index_col, rows):
    lane = lax.broadcasted_iota(I32, (rows, LANES), 1)
    hit = (index_col & (LANES - 1)) == lane
    return jnp.where(hit, (index_col >> 7).astype(F32), -1.0)


def lane_code(index_col, rows):
    return lane_code_f32(index_col, rows).astype(BF16)


def expand(code, first, count):
    one = jnp.ones((), BF16)
    zero = jnp.zeros((), BF16)
    return jnp.concatenate(
        [jnp.where(code == jnp.asarray(k, BF16), one, zero) for k in range(first, first + count)],
        axis=1,
    )


def plan_kernel(cap, ocap, node_dev, source_ref, ids_ref, pcode_ref):
    batches, events = source_ref.shape
    rows = ids_ref.shape[1]
    per = cap + ocap
    group_nodes = rows * node_dev
    upper = (
        lax.broadcasted_iota(I32, (events, events), 0)
        <= lax.broadcasted_iota(I32, (events, events), 1)
    ).astype(F32).astype(BF16)
    bucket_iota = lax.broadcasted_iota(I32, (2 * rows, events), 0)
    lane_iota = lax.broadcasted_iota(I32, (LANES, events), 0)
    high = jnp.zeros((rows, LANES), F32)
    low = jnp.zeros((rows, LANES), F32)
    places = []
    for b in range(batches):
        src = source_ref[b : b + 1, :]
        far = src >= group_nodes
        local = jnp.where(far, src - group_nodes, src)
        dest = local // node_dev
        offset = local - dest * node_dev
        bucket = jnp.where(far, dest + rows, dest)
        hit = bucket == bucket_iota
        hitf = hit.astype(F32)
        running = dot(hitf.astype(BF16), upper)
        rank = jnp.sum(hitf * running, axis=0, keepdims=True).astype(I32) - 1
        slot = jnp.where(far, rank + cap, rank)
        both = (hitf[:rows] + hitf[rows:]).astype(BF16)
        spot = (slot + b * per == lane_iota).astype(F32)
        high = high + dot_nt(both, (spot * (offset >> 6).astype(F32)).astype(BF16))
        low = low + dot_nt(both, (spot * (offset & 63).astype(F32)).astype(BF16))
        places.append(dest * per + slot)
    ids = high.astype(I32) * 64 + low.astype(I32)
    for g in range(ids_ref.shape[0]):
        ids_ref[g] = ids
    stacked = jnp.concatenate(
        [p.astype(F32) for p in places] + [jnp.zeros((LANES - batches, events), F32)], axis=0
    )
    cols = stacked.T
    for b in range(batches):
        pcode_ref[b] = lane_code(cols[:, b : b + 1].astype(I32), events)


def spread_codes(ids, first, count):
    rows = ids.shape[0]
    total = rows * count
    place = lax.broadcasted_iota(I32, (total, LANES), 0)
    lane = lax.broadcasted_iota(I32, (total, LANES), 1)
    row = place // count
    copy = (row[:, :rows] == lane[:, :rows]).astype(F32).astype(BF16)
    keep = (lane == first + place - row * count).astype(F32)
    ones = jnp.ones((LANES, LANES), BF16)

    def everywhere(part):
        taken = dot(copy, part.astype(F32).astype(BF16)) * keep
        return dot(taken.astype(BF16), ones)

    low = everywhere(ids & (LANES - 1))
    high = everywhere(ids >> 7)
    return jnp.where(low == lane.astype(F32), high, -1.0).astype(BF16)


def code_kernel(cap, per, at_ref, asked_ref, _, own_ref, far_ref):
    b = at_ref[0]
    groups, rows, _ = asked_ref.shape
    own_ref[...] = spread_codes(asked_ref[at_ref[1]], b * per, per)
    block = rows * (per - cap)
    for g in range(groups):
        far_ref[g * block : (g + 1) * block, :] = spread_codes(
            asked_ref[g], b * per + cap, per - cap
        )


def cosine(x):
    turns = jnp.floor(x * 0.15915494309189535 + 0.5)
    r = (x - turns * 6.28125) - turns * 0.0019353071795864769
    z = r * r
    value = jnp.full_like(z, 1.0 / 20922789888000.0)
    for factor in (
        -1.0 / 87178291200.0,
        1.0 / 479001600.0,
        -1.0 / 3628800.0,
        1.0 / 40320.0,
        -1.0 / 720.0,
        1.0 / 24.0,
        -0.5,
        1.0,
    ):
        value = value * z + factor
    return value


def prep_kernel(
    width,
    at_ref,
    target_ref,
    time_ref,
    node_time_ref,
    edge_ref,
    freq_ref,
    phase_ref,
    w_ref,
    _,
    base_ref,
    gcode_ref,
    scode_ref,
    same_ref,
    count_ref,
):
    b = at_ref[0]
    batches, events = target_ref.shape
    node_dev = node_time_ref.shape[1]
    enc_at = 2 * width
    edge_at = enc_at + freq_ref.shape[1]
    trow = target_ref[pl.ds(b, 1), :]
    erow = time_ref[pl.ds(b, 1), :]
    stacked = jnp.concatenate(
        [trow.astype(F32), erow.astype(F32), jnp.zeros((LANES - 2, events), F32)], axis=0
    )
    cols = stacked.T
    sub = lax.broadcasted_iota(I32, (events, events), 0)
    lane = lax.broadcasted_iota(I32, (events, events), 1)
    node_lane = lax.broadcasted_iota(I32, (events, node_dev), 1)
    tcol = cols[:, 0:1].astype(I32)
    ecol = cols[:, 1:2]
    seen = jnp.max(
        jnp.where(tcol == node_lane, node_time_ref[...].astype(F32), 0.0), axis=1, keepdims=True
    )
    for before in range(batches - 1):
        row = target_ref[before : before + 1, :]
        row = jnp.where((row < 0) | (before >= b), -2, row)
        seen = jnp.maximum(
            seen,
            jnp.max(
                jnp.where(tcol == row, time_ref[before : before + 1, :].astype(F32), 0.0),
                axis=1,
                keepdims=True,
            ),
        )
    angle = (ecol - seen) * freq_ref[...] + phase_ref[...]
    encoded = cosine(angle).astype(BF16)
    base_ref[...] = dot(encoded, w_ref[enc_at:edge_at, :]) + dot(edge_ref[0], w_ref[edge_at:, :])
    gcode_ref[...] = lane_code(tcol, events)
    same = (tcol == trow) & (trow >= 0)
    samef = same.astype(F32)
    same_ref[...] = samef.astype(BF16)
    count_ref[...] = jnp.broadcast_to(
        jnp.maximum(jnp.sum(samef, axis=1, keepdims=True), 1.0), (events, LANES)
    )
    earlier = jnp.max(jnp.where(sub < lane, samef, 0.0), axis=0, keepdims=True)
    first = jnp.where(earlier > 0.0, -1, trow)
    sub128 = lax.broadcasted_iota(I32, (LANES, events), 0)
    scode_ref[...] = jnp.where(
        (first & (LANES - 1)) == sub128, (first >> 7).astype(F32), -1.0
    ).astype(BF16)


def serve_rows(table_ref, code_ref, out_ref, step):
    blocks = table_ref.shape[0] // LANES
    table = table_ref[...]
    for start in range(0, code_ref.shape[0], step):
        picked = dot(expand(code_ref[start : start + step, :], 0, blocks), table)
        out_ref[start : start + step, :] = picked.astype(BF16)


def serve_kernel(table_ref, own_code_ref, far_code_ref, own_ref, far_ref):
    serve_rows(table_ref, own_code_ref, own_ref, 256)
    serve_rows(table_ref, far_code_ref, far_ref, 512)


def local_kernel(table_ref, gcode_ref, base_ref, w_ref, mem_ref, out_ref):
    blocks = table_ref.shape[0] // LANES
    mem = dot(expand(gcode_ref[...], 0, blocks), table_ref[...]).astype(BF16)
    mem_ref[...] = mem
    out_ref[...] = base_ref[...] + dot(mem, w_ref[: mem.shape[1], :])


def update_kernel(
    last,
    at_ref,
    table_ref,
    back_ref,
    pcode_ref,
    base_ref,
    mem_ref,
    same_ref,
    count_ref,
    scode_ref,
    w_ref,
    w_input_ref,
    w_hidden_ref,
    bias_input_ref,
    bias_hidden_ref,
    own_code_ref,
    far_code_ref,
    new_ref,
    own_out_ref,
    far_out_ref,
):
    width = table_ref.shape[1]
    mem = mem_ref[...]
    hidden = dot(mem, w_hidden_ref[...]) + bias_hidden_ref[...]
    source = dot(expand(pcode_ref[0], 0, back_ref.shape[0] // LANES), back_ref[...])
    w_source = w_ref[width : 2 * width, :]
    message = (base_ref[...] + dot(source.astype(BF16), w_source)).astype(BF16)
    total = dot(same_ref[...], message)
    averaged = (total / count_ref[:, :1]).astype(BF16)
    gates = dot(averaged, w_input_ref[...]) + bias_input_ref[...]
    reset = jax.nn.sigmoid(gates[:, :width] + hidden[:, :width])
    update = jax.nn.sigmoid(gates[:, width : 2 * width] + hidden[:, width : 2 * width])
    candidate = jnp.tanh(gates[:, 2 * width :] + reset * hidden[:, 2 * width :])
    fresh = ((1.0 - update) * candidate + update * mem.astype(F32)).astype(BF16)
    ones = jnp.ones((fresh.shape[0], LANES), BF16)
    placed = jnp.concatenate([fresh, ones], axis=1)
    scode = scode_ref[...]
    one = jnp.ones((), BF16)
    zero = jnp.zeros((), BF16)
    blocks = table_ref.shape[0] // LANES
    group = 4
    for k in range(0, blocks, group):
        spread = jnp.concatenate(
            [jnp.where(scode == jnp.asarray(k + j, BF16), one, zero) for j in range(group)], axis=0
        )
        moved = dot(spread, placed)
        rows = slice(k * LANES, (k + group) * LANES)
        new_ref[rows, :] = jnp.where(
            moved[:, width : width + 1] > 0.0, moved[:, :width], table_ref[rows, :].astype(F32)
        ).astype(BF16)

    @pl.when(at_ref[0] < last)
    def _():
        serve_rows(new_ref, own_code_ref, own_out_ref, 256)
        serve_rows(new_ref, far_code_ref, far_out_ref, 512)


def from_owner(own_rows, far_rows, owner, cap):
    rows, _, width = own_rows.shape
    ys = far_rows.shape[0] // 2

    def branch(root):
        y, z = root // 2, root % 2

        def body(own_rows, far_rows):
            me = lax.axis_index("dom")
            my_y, my_z = me >> 1, me & 1

            def spread(which):
                part = far_rows[2 * y + which]
                moved = []
                for shift in range(1, ys):
                    there = (y + shift) % ys
                    pair = (root, 2 * there + z)
                    moved.append((there, lax.ppermute(far_rows[2 * there + which], "dom", [pair])))
                for there, block in moved:
                    part = jnp.where(my_y == there, block, part)
                return part

            across = lax.ppermute(
                spread(1 - z), "dom", [(2 * i + z, 2 * i + 1 - z) for i in range(ys)]
            )
            mine = jnp.where(my_z == z, spread(z), across)
            return own_rows.at[:, cap:, :].set(mine.reshape(rows, -1, width))

        return body

    return lax.switch(owner, [branch(r) for r in range(2 * ys)], own_rows, far_rows)


def shards(
    memory,
    node_time,
    target,
    source,
    event_time,
    edge_feat,
    owner_group,
    w_message,
    frequency,
    phase_shift,
    w_input,
    w_hidden,
    bias_input,
    bias_hidden,
):
    node_dev, width = memory.shape
    batches, events = target.shape
    rows = lax.axis_size("row")
    groups = lax.axis_size("dom")
    cap = 3 * events // (2 * rows)
    ocap = events // (2 * rows)
    per = cap + ocap
    shape = jax.ShapeDtypeStruct
    code = shape((events, LANES), BF16)

    ids, pcode = call(
        functools.partial(plan_kernel, cap, ocap, node_dev),
        (shape((groups, rows, batches * per), I32), shape((batches, events, LANES), BF16)),
        (source,),
        name="plan",
    )
    asked = lax.all_to_all(
        ids.reshape(groups * rows, 1, batches * per), ("dom", "row"), 0, 0, tiled=True
    ).reshape(groups, rows, batches * per)
    me = lax.axis_index("dom").astype(I32)
    times_row = node_time.reshape(1, node_dev)
    freq_row = frequency.reshape(1, -1)
    phase_row = phase_shift.reshape(1, -1)
    input_row = bias_input.reshape(1, -1)
    hidden_row = bias_hidden.reshape(1, -1)
    anywhere = pl.BlockSpec(memory_space=pl.ANY)

    def codes(b, after):
        return call(
            functools.partial(code_kernel, cap, per),
            (
                shape((rows * per, LANES), BF16),
                shape((groups * rows * ocap, LANES), BF16),
            ),
            (asked, after),
            flops=2 * 10**9,
            name="codes",
            specs={1: anywhere},
            scalars=(jnp.stack([b, me]),),
        )

    own_shape = shape((rows * per, width), BF16)
    far_shape = shape((groups * rows * ocap, width), BF16)
    own_rows, far_rows = call(
        serve_kernel,
        (own_shape, far_shape),
        (memory,) + tuple(codes(jnp.zeros((), I32), asked)),
        flops=4 * 10**9,
        name="serve",
    )

    def batch(b, carry):
        table, own_rows, far_rows = carry
        at = b.reshape(1)
        sent = from_owner(
            own_rows.reshape(rows, per, width),
            far_rows.reshape(groups, rows * ocap, width),
            lax.dynamic_index_in_dim(owner_group, b, 0, keepdims=False),
            cap,
        )
        back = lax.all_to_all(sent, "row", 0, 0, tiled=True).reshape(rows * per, width)
        base, gcode, scode, same, count = call(
            functools.partial(prep_kernel, width),
            (
                shape((events, width), F32),
                code,
                shape((LANES, events), BF16),
                shape((events, events), BF16),
                shape((events, LANES), F32),
            ),
            (target, event_time, times_row, edge_feat, freq_row, phase_row, w_message, sent),
            flops=3 * 10**9,
            name="prep",
            specs={
                3: pl.BlockSpec((1,) + edge_feat.shape[1:], lambda i, at: (at[0], 0, 0)),
                7: anywhere,
            },
            scalars=(at,),
        )
        mem, local = call(
            local_kernel,
            (shape((events, width), BF16), shape((events, width), F32)),
            (table, gcode, base, w_message),
            flops=3 * 10**9,
            name="local",
        )
        own_code, far_code = codes(b + 1, sent)
        return call(
            functools.partial(update_kernel, batches - 1),
            (shape((node_dev, width), BF16), own_shape, far_shape),
            (
                table,
                back,
                pcode,
                local,
                mem,
                same,
                count,
                scode,
                w_message,
                w_input,
                w_hidden,
                input_row,
                hidden_row,
                own_code,
                far_code,
            ),
            flops=6 * 10**9,
            name="update",
            specs={2: pl.BlockSpec((1, events, LANES), lambda i, at: (at[0], 0, 0))},
            scalars=(at,),
        )

    return lax.fori_loop(0, batches, batch, (memory, own_rows, far_rows))[0]


def solution(mesh):
    in_specs = (
        P(("dom", "row"), None),
        P(("dom", "row")),
        P(None, ("dom", "row")),
        P(None, ("dom", "row")),
        P(None, ("dom", "row")),
        P(None, ("dom", "row"), None),
        P(),
        P(),
        P(),
        P(),
        P(),
        P(),
        P(),
        P(),
    )
    out_specs = P(("dom", "row"), None)
    return jax.shard_map(shards, mesh=mesh, in_specs=in_specs, out_specs=out_specs, check_vma=False)
```

```python
import functools

import jax
import jax.numpy as jnp
from jax import lax
from jax.experimental import pallas as pl
from jax.experimental.pallas import tpu as pltpu
from jax.sharding import PartitionSpec as P

LANES = 128
F32 = jnp.float32
BF16 = jnp.bfloat16
I32 = jnp.int32
MIB = 1024 * 1024
VMEM_MIB = dict(plan=6, codes=6, prep=8, local=8, serve=8, update=16)


def whole():
    return pl.BlockSpec(memory_space=pltpu.VMEM)


def call(kernel, out_shape, args, flops=0, name=None, specs=None, scalars=(), aliases=None):
    moved = sum(a.size * a.dtype.itemsize for a in args)
    moved += sum(o.size * o.dtype.itemsize for o in jax.tree.leaves(out_shape))
    specs = specs or {}
    return pl.pallas_call(
        kernel,
        out_shape=out_shape,
        grid_spec=pltpu.PrefetchScalarGridSpec(
            num_scalar_prefetch=len(scalars),
            grid=(1,) if scalars else (),
            in_specs=[specs.get(i, whole()) for i in range(len(args))],
            out_specs=jax.tree.map(lambda _: whole(), out_shape),
        ),
        input_output_aliases=aliases or {},
        compiler_params=pltpu.CompilerParams(vmem_limit_bytes=VMEM_MIB[name] * MIB),
        cost_estimate=pl.CostEstimate(flops=flops, bytes_accessed=moved, transcendentals=0),
        name=name,
    )(*scalars, *args)


def dot(a, b):
    return jnp.dot(a, b, preferred_element_type=F32)


def dot_nt(a, b):
    return lax.dot_general(a, b, (((1,), (1,)), ((), ())), preferred_element_type=F32)


def lane_code_f32(index_col, rows):
    lane = lax.broadcasted_iota(I32, (rows, LANES), 1)
    hit = (index_col & (LANES - 1)) == lane
    return jnp.where(hit, (index_col >> 7).astype(F32), -1.0)


def lane_code(index_col, rows):
    return lane_code_f32(index_col, rows).astype(BF16)


def expand(code, first, count):
    one = jnp.ones((), BF16)
    zero = jnp.zeros((), BF16)
    return jnp.concatenate(
        [jnp.where(code == jnp.asarray(k, BF16), one, zero) for k in range(first, first + count)],
        axis=1,
    )


def plan_kernel(cap, ocap, node_dev, source_ref, ids_ref, pcode_ref):
    batches, events = source_ref.shape
    rows = ids_ref.shape[1]
    per = cap + ocap
    group_nodes = rows * node_dev
    upper = (
        lax.broadcasted_iota(I32, (events, events), 0)
        <= lax.broadcasted_iota(I32, (events, events), 1)
    ).astype(F32).astype(BF16)
    bucket_iota = lax.broadcasted_iota(I32, (2 * rows, events), 0)
    lane_iota = lax.broadcasted_iota(I32, (LANES, events), 0)
    high = jnp.zeros((rows, LANES), F32)
    low = jnp.zeros((rows, LANES), F32)
    places = []
    for b in range(batches):
        src = source_ref[b : b + 1, :]
        far = src >= group_nodes
        local = jnp.where(far, src - group_nodes, src)
        dest = local // node_dev
        offset = local - dest * node_dev
        bucket = jnp.where(far, dest + rows, dest)
        hit = bucket == bucket_iota
        hitf = hit.astype(F32)
        running = dot(hitf.astype(BF16), upper)
        rank = jnp.sum(hitf * running, axis=0, keepdims=True).astype(I32) - 1
        slot = jnp.where(far, rank + cap, rank)
        both = (hitf[:rows] + hitf[rows:]).astype(BF16)
        spot = (slot + b * per == lane_iota).astype(F32)
        high = high + dot_nt(both, (spot * (offset >> 6).astype(F32)).astype(BF16))
        low = low + dot_nt(both, (spot * (offset & 63).astype(F32)).astype(BF16))
        places.append(dest * per + slot)
    ids = high.astype(I32) * 64 + low.astype(I32)
    for g in range(ids_ref.shape[0]):
        ids_ref[g] = ids
    stacked = jnp.concatenate(
        [p.astype(F32) for p in places] + [jnp.zeros((LANES - batches, events), F32)], axis=0
    )
    cols = stacked.T
    for b in range(batches):
        pcode_ref[b] = lane_code(cols[:, b : b + 1].astype(I32), events)


def spread_codes(ids, first, count):
    rows = ids.shape[0]
    total = rows * count
    place = lax.broadcasted_iota(I32, (total, LANES), 0)
    lane = lax.broadcasted_iota(I32, (total, LANES), 1)
    row = place // count
    copy = (row[:, :rows] == lane[:, :rows]).astype(F32).astype(BF16)
    keep = (lane == first + place - row * count).astype(F32)
    ones = jnp.ones((LANES, LANES), BF16)

    def everywhere(part):
        taken = dot(copy, part.astype(F32).astype(BF16)) * keep
        return dot(taken.astype(BF16), ones)

    low = everywhere(ids & (LANES - 1))
    high = everywhere(ids >> 7)
    return jnp.where(low == lane.astype(F32), high, -1.0).astype(BF16)


def code_kernel(cap, per, at_ref, asked_ref, _, own_ref, far_ref):
    b = at_ref[0]
    groups, rows, _ = asked_ref.shape
    own_ref[...] = spread_codes(asked_ref[at_ref[1]], b * per, per)
    block = rows * (per - cap)
    for g in range(groups):
        far_ref[g * block : (g + 1) * block, :] = spread_codes(
            asked_ref[g], b * per + cap, per - cap
        )


def cosine(x):
    turns = jnp.floor(x * 0.15915494309189535 + 0.5)
    r = (x - turns * 6.28125) - turns * 0.0019353071795864769
    z = r * r
    value = jnp.full_like(z, 1.0 / 20922789888000.0)
    for factor in (
        -1.0 / 87178291200.0,
        1.0 / 479001600.0,
        -1.0 / 3628800.0,
        1.0 / 40320.0,
        -1.0 / 720.0,
        1.0 / 24.0,
        -0.5,
        1.0,
    ):
        value = value * z + factor
    return value


def prep_kernel(
    width,
    at_ref,
    target_ref,
    time_ref,
    node_time_ref,
    edge_ref,
    freq_ref,
    phase_ref,
    w_ref,
    _,
    base_ref,
    gcode_ref,
    scode_ref,
    same_ref,
    count_ref,
):
    b = at_ref[0]
    batches, events = target_ref.shape
    node_dev = node_time_ref.shape[1]
    enc_at = 2 * width
    edge_at = enc_at + freq_ref.shape[1]
    trow = target_ref[pl.ds(b, 1), :]
    erow = time_ref[pl.ds(b, 1), :]
    stacked = jnp.concatenate(
        [trow.astype(F32), erow.astype(F32), jnp.zeros((LANES - 2, events), F32)], axis=0
    )
    cols = stacked.T
    sub = lax.broadcasted_iota(I32, (events, events), 0)
    lane = lax.broadcasted_iota(I32, (events, events), 1)
    node_lane = lax.broadcasted_iota(I32, (events, node_dev), 1)
    tcol = cols[:, 0:1].astype(I32)
    ecol = cols[:, 1:2]
    seen = jnp.max(
        jnp.where(tcol == node_lane, node_time_ref[...].astype(F32), 0.0), axis=1, keepdims=True
    )
    for before in range(batches - 1):
        row = target_ref[before : before + 1, :]
        row = jnp.where((row < 0) | (before >= b), -2, row)
        seen = jnp.maximum(
            seen,
            jnp.max(
                jnp.where(tcol == row, time_ref[before : before + 1, :].astype(F32), 0.0),
                axis=1,
                keepdims=True,
            ),
        )
    angle = (ecol - seen) * freq_ref[...] + phase_ref[...]
    encoded = cosine(angle).astype(BF16)
    base_ref[...] = dot(encoded, w_ref[enc_at:edge_at, :]) + dot(edge_ref[0], w_ref[edge_at:, :])
    gcode_ref[...] = lane_code(tcol, events)
    same = (tcol == trow) & (trow >= 0)
    samef = same.astype(F32)
    same_ref[...] = samef.astype(BF16)
    count_ref[...] = jnp.broadcast_to(
        jnp.maximum(jnp.sum(samef, axis=1, keepdims=True), 1.0), (events, LANES)
    )
    earlier = jnp.max(jnp.where(sub < lane, samef, 0.0), axis=0, keepdims=True)
    first = jnp.where(earlier > 0.0, -1, trow)
    sub128 = lax.broadcasted_iota(I32, (LANES, events), 0)
    scode_ref[...] = jnp.where(
        (first & (LANES - 1)) == sub128, (first >> 7).astype(F32), -1.0
    ).astype(BF16)


def serve_rows(table_ref, code_ref, out_ref, step):
    blocks = table_ref.shape[0] // LANES
    table = table_ref[...]
    for start in range(0, code_ref.shape[0], step):
        picked = dot(expand(code_ref[start : start + step, :], 0, blocks), table)
        out_ref[start : start + step, :] = picked.astype(BF16)


def serve_kernel(table_ref, own_code_ref, far_code_ref, own_ref, far_ref):
    serve_rows(table_ref, own_code_ref, own_ref, 256)
    serve_rows(table_ref, far_code_ref, far_ref, 512)


def local_kernel(table_ref, gcode_ref, base_ref, w_ref, mem_ref, out_ref):
    blocks = table_ref.shape[0] // LANES
    mem = dot(expand(gcode_ref[...], 0, blocks), table_ref[...]).astype(BF16)
    mem_ref[...] = mem
    out_ref[...] = base_ref[...] + dot(mem, w_ref[: mem.shape[1], :])


def update_kernel(
    last,
    at_ref,
    table_ref,
    back_ref,
    pcode_ref,
    base_ref,
    mem_ref,
    same_ref,
    count_ref,
    scode_ref,
    w_ref,
    w_input_ref,
    w_hidden_ref,
    bias_input_ref,
    bias_hidden_ref,
    own_code_ref,
    far_code_ref,
    new_ref,
    own_out_ref,
    far_out_ref,
):
    width = table_ref.shape[1]
    mem = mem_ref[...]
    hidden = dot(mem, w_hidden_ref[...]) + bias_hidden_ref[...]
    source = dot(expand(pcode_ref[0], 0, back_ref.shape[0] // LANES), back_ref[...])
    w_source = w_ref[width : 2 * width, :]
    message = (base_ref[...] + dot(source.astype(BF16), w_source)).astype(BF16)
    total = dot(same_ref[...], message)
    averaged = (total / count_ref[:, :1]).astype(BF16)
    gates = dot(averaged, w_input_ref[...]) + bias_input_ref[...]
    reset = jax.nn.sigmoid(gates[:, :width] + hidden[:, :width])
    update = jax.nn.sigmoid(gates[:, width : 2 * width] + hidden[:, width : 2 * width])
    candidate = jnp.tanh(gates[:, 2 * width :] + reset * hidden[:, 2 * width :])
    fresh = ((1.0 - update) * candidate + update * mem.astype(F32)).astype(BF16)
    ones = jnp.ones((fresh.shape[0], LANES), BF16)
    placed = jnp.concatenate([fresh, ones], axis=1)
    scode = scode_ref[...]
    one = jnp.ones((), BF16)
    zero = jnp.zeros((), BF16)
    blocks = table_ref.shape[0] // LANES
    group = 4
    for k in range(0, blocks, group):
        spread = jnp.concatenate(
            [jnp.where(scode == jnp.asarray(k + j, BF16), one, zero) for j in range(group)], axis=0
        )
        moved = dot(spread, placed)
        rows = slice(k * LANES, (k + group) * LANES)
        new_ref[rows, :] = jnp.where(
            moved[:, width : width + 1] > 0.0, moved[:, :width], table_ref[rows, :].astype(F32)
        ).astype(BF16)

    @pl.when(at_ref[0] < last)
    def _():
        serve_rows(new_ref, own_code_ref, own_out_ref, 256)
        serve_rows(new_ref, far_code_ref, far_out_ref, 512)


def from_owner(own_rows, far_rows, owner, cap):
    rows, _, width = own_rows.shape
    ys = far_rows.shape[0] // 2

    def branch(root):
        y, z = root // 2, root % 2

        def body(own_rows, far_rows):
            me = lax.axis_index("dom")
            my_y, my_z = me >> 1, me & 1

            def spread(which):
                part = far_rows[2 * y + which]
                moved = []
                for shift in range(1, ys):
                    there = (y + shift) % ys
                    pairs = [(2 * y + side, 2 * there + side) for side in range(2)]
                    block = lax.ppermute(far_rows[2 * there + which], "dom", pairs)
                    moved.append((there, block))
                for there, block in moved:
                    part = jnp.where(my_y == there, block, part)
                return part

            across = lax.ppermute(
                spread(1 - z), "dom", [(2 * i + z, 2 * i + 1 - z) for i in range(ys)]
            )
            mine = jnp.where(my_z == z, spread(z), across)
            return own_rows.at[:, cap:, :].set(mine.reshape(rows, -1, width))

        return body

    return lax.switch(owner, [branch(r) for r in range(2 * ys)], own_rows, far_rows)


def shards(
    memory,
    node_time,
    target,
    source,
    event_time,
    edge_feat,
    owner_group,
    w_message,
    frequency,
    phase_shift,
    w_input,
    w_hidden,
    bias_input,
    bias_hidden,
):
    node_dev, width = memory.shape
    batches, events = target.shape
    rows = lax.axis_size("row")
    groups = lax.axis_size("dom")
    cap = 3 * events // (2 * rows)
    ocap = events // (2 * rows)
    per = cap + ocap
    shape = jax.ShapeDtypeStruct
    code = shape((events, LANES), BF16)

    ids, pcode = call(
        functools.partial(plan_kernel, cap, ocap, node_dev),
        (shape((groups, rows, batches * per), I32), shape((batches, events, LANES), BF16)),
        (source,),
        name="plan",
    )
    asked = lax.all_to_all(
        ids.reshape(groups * rows, 1, batches * per), ("dom", "row"), 0, 0, tiled=True
    ).reshape(groups, rows, batches * per)
    me = lax.axis_index("dom").astype(I32)
    times_row = node_time.reshape(1, node_dev)
    freq_row = frequency.reshape(1, -1)
    phase_row = phase_shift.reshape(1, -1)
    input_row = bias_input.reshape(1, -1)
    hidden_row = bias_hidden.reshape(1, -1)
    anywhere = pl.BlockSpec(memory_space=pl.ANY)

    def codes(b, after):
        return call(
            functools.partial(code_kernel, cap, per),
            (
                shape((rows * per, LANES), BF16),
                shape((groups * rows * ocap, LANES), BF16),
            ),
            (asked, after),
            flops=2 * 10**9,
            name="codes",
            specs={1: anywhere},
            scalars=(jnp.stack([b, me]),),
        )

    own_shape = shape((rows * per, width), BF16)
    far_shape = shape((groups * rows * ocap, width), BF16)
    own_rows, far_rows = call(
        serve_kernel,
        (own_shape, far_shape),
        (memory,) + tuple(codes(jnp.zeros((), I32), asked)),
        flops=4 * 10**9,
        name="serve",
    )

    def batch(b, carry):
        table, own_rows, far_rows = carry
        at = b.reshape(1)
        sent = from_owner(
            own_rows.reshape(rows, per, width),
            far_rows.reshape(groups, rows * ocap, width),
            lax.dynamic_index_in_dim(owner_group, b, 0, keepdims=False),
            cap,
        )
        back = lax.all_to_all(sent, "row", 0, 0, tiled=True).reshape(rows * per, width)
        base, gcode, scode, same, count = call(
            functools.partial(prep_kernel, width),
            (
                shape((events, width), F32),
                code,
                shape((LANES, events), BF16),
                shape((events, events), BF16),
                shape((events, LANES), F32),
            ),
            (target, event_time, times_row, edge_feat, freq_row, phase_row, w_message, sent),
            flops=3 * 10**9,
            name="prep",
            specs={
                3: pl.BlockSpec((1,) + edge_feat.shape[1:], lambda i, at: (at[0], 0, 0)),
                7: anywhere,
            },
            scalars=(at,),
        )
        mem, local = call(
            local_kernel,
            (shape((events, width), BF16), shape((events, width), F32)),
            (table, gcode, base, w_message),
            flops=3 * 10**9,
            name="local",
        )
        own_code, far_code = codes(b + 1, sent)
        return call(
            functools.partial(update_kernel, batches - 1),
            (shape((node_dev, width), BF16), own_shape, far_shape),
            (
                table,
                back,
                pcode,
                local,
                mem,
                same,
                count,
                scode,
                w_message,
                w_input,
                w_hidden,
                input_row,
                hidden_row,
                own_code,
                far_code,
            ),
            flops=6 * 10**9,
            name="update",
            specs={2: pl.BlockSpec((1, events, LANES), lambda i, at: (at[0], 0, 0))},
            scalars=(at,),
        )

    return lax.fori_loop(0, batches, batch, (memory, own_rows, far_rows))[0]


def solution(mesh):
    in_specs = (
        P(("dom", "row"), None),
        P(("dom", "row")),
        P(None, ("dom", "row")),
        P(None, ("dom", "row")),
        P(None, ("dom", "row")),
        P(None, ("dom", "row"), None),
        P(),
        P(),
        P(),
        P(),
        P(),
        P(),
        P(),
        P(),
    )
    out_specs = P(("dom", "row"), None)
    return jax.shard_map(shards, mesh=mesh, in_specs=in_specs, out_specs=out_specs, check_vma=False)
```

```python
import functools

import jax
import jax.numpy as jnp
from jax import lax
from jax.experimental import pallas as pl
from jax.experimental.pallas import tpu as pltpu
from jax.sharding import PartitionSpec as P

LANES = 128
F32 = jnp.float32
BF16 = jnp.bfloat16
I32 = jnp.int32
MIB = 1024 * 1024
VMEM_MIB = dict(plan=6, codes=6, prep=8, local=8, serve=8, update=16)


def whole():
    return pl.BlockSpec(memory_space=pltpu.VMEM)


def call(kernel, out_shape, args, flops=0, name=None, specs=None, scalars=(), aliases=None):
    moved = sum(a.size * a.dtype.itemsize for a in args)
    moved += sum(o.size * o.dtype.itemsize for o in jax.tree.leaves(out_shape))
    specs = specs or {}
    return pl.pallas_call(
        kernel,
        out_shape=out_shape,
        grid_spec=pltpu.PrefetchScalarGridSpec(
            num_scalar_prefetch=len(scalars),
            grid=(1,) if scalars else (),
            in_specs=[specs.get(i, whole()) for i in range(len(args))],
            out_specs=jax.tree.map(lambda _: whole(), out_shape),
        ),
        input_output_aliases=aliases or {},
        compiler_params=pltpu.CompilerParams(vmem_limit_bytes=VMEM_MIB[name] * MIB),
        cost_estimate=pl.CostEstimate(flops=flops, bytes_accessed=moved, transcendentals=0),
        name=name,
    )(*scalars, *args)


def dot(a, b):
    return jnp.dot(a, b, preferred_element_type=F32)


def dot_nt(a, b):
    return lax.dot_general(a, b, (((1,), (1,)), ((), ())), preferred_element_type=F32)


def lane_code_f32(index_col, rows):
    lane = lax.broadcasted_iota(I32, (rows, LANES), 1)
    hit = (index_col & (LANES - 1)) == lane
    return jnp.where(hit, (index_col >> 7).astype(F32), -1.0)


def lane_code(index_col, rows):
    return lane_code_f32(index_col, rows).astype(BF16)


def expand(code, first, count):
    one = jnp.ones((), BF16)
    zero = jnp.zeros((), BF16)
    return jnp.concatenate(
        [jnp.where(code == jnp.asarray(k, BF16), one, zero) for k in range(first, first + count)],
        axis=1,
    )


def plan_kernel(cap, ocap, node_dev, flip_ref, source_ref, ids_ref, pcode_ref):
    batches, events = source_ref.shape
    rows = ids_ref.shape[1]
    per = cap + ocap
    group_nodes = rows * node_dev
    upper = (
        lax.broadcasted_iota(I32, (events, events), 0)
        <= lax.broadcasted_iota(I32, (events, events), 1)
    ).astype(F32).astype(BF16)
    bucket_iota = lax.broadcasted_iota(I32, (2 * rows, events), 0)
    lane_iota = lax.broadcasted_iota(I32, (LANES, events), 0)
    high = jnp.zeros((rows, LANES), F32)
    low = jnp.zeros((rows, LANES), F32)
    places = []
    for b in range(batches):
        src = source_ref[b : b + 1, :]
        far = src >= group_nodes
        local = jnp.where(far, src - group_nodes, src)
        dest = local // node_dev
        offset = local - dest * node_dev
        bucket = jnp.where(far, dest + rows, dest)
        hit = bucket == bucket_iota
        hitf = hit.astype(F32)
        running = dot(hitf.astype(BF16), upper)
        rank = jnp.sum(hitf * running, axis=0, keepdims=True).astype(I32) - 1
        slot = jnp.where(far, rank + cap, rank)
        both = (hitf[:rows] + hitf[rows:]).astype(BF16)
        spot = (slot + b * per == lane_iota).astype(F32)
        high = high + dot_nt(both, (spot * (offset >> 6).astype(F32)).astype(BF16))
        low = low + dot_nt(both, (spot * (offset & 63).astype(F32)).astype(BF16))
        places.append(jnp.where(far, dest ^ flip_ref[b], dest) * per + slot)
    ids = high.astype(I32) * 64 + low.astype(I32)
    for g in range(ids_ref.shape[0]):
        ids_ref[g] = ids
    stacked = jnp.concatenate(
        [p.astype(F32) for p in places] + [jnp.zeros((LANES - batches, events), F32)], axis=0
    )
    cols = stacked.T
    for b in range(batches):
        pcode_ref[b] = lane_code(cols[:, b : b + 1].astype(I32), events)


def spread_codes(ids, first, count):
    rows = ids.shape[0]
    total = rows * count
    place = lax.broadcasted_iota(I32, (total, LANES), 0)
    lane = lax.broadcasted_iota(I32, (total, LANES), 1)
    row = place // count
    copy = (row[:, :rows] == lane[:, :rows]).astype(F32).astype(BF16)
    keep = (lane == first + place - row * count).astype(F32)
    ones = jnp.ones((LANES, LANES), BF16)

    def everywhere(part):
        taken = dot(copy, part.astype(F32).astype(BF16)) * keep
        return dot(taken.astype(BF16), ones)

    low = everywhere(ids & (LANES - 1))
    high = everywhere(ids >> 7)
    return jnp.where(low == lane.astype(F32), high, -1.0).astype(BF16)


def code_kernel(cap, per, at_ref, asked_ref, _, own_ref, far_ref):
    b = at_ref[0]
    groups, rows, _ = asked_ref.shape
    own_ref[...] = spread_codes(asked_ref[at_ref[1]], b * per, per)
    block = rows * (per - cap)
    for g in range(groups):
        far_ref[g * block : (g + 1) * block, :] = spread_codes(
            asked_ref[g], b * per + cap, per - cap
        )


def cosine(x):
    turns = jnp.floor(x * 0.15915494309189535 + 0.5)
    r = (x - turns * 6.28125) - turns * 0.0019353071795864769
    z = r * r
    value = jnp.full_like(z, 1.0 / 20922789888000.0)
    for factor in (
        -1.0 / 87178291200.0,
        1.0 / 479001600.0,
        -1.0 / 3628800.0,
        1.0 / 40320.0,
        -1.0 / 720.0,
        1.0 / 24.0,
        -0.5,
        1.0,
    ):
        value = value * z + factor
    return value


def prep_kernel(
    width,
    at_ref,
    target_ref,
    time_ref,
    node_time_ref,
    edge_ref,
    freq_ref,
    phase_ref,
    w_ref,
    _,
    base_ref,
    gcode_ref,
    scode_ref,
    same_ref,
):
    b = at_ref[0]
    batches, events = target_ref.shape
    node_dev = node_time_ref.shape[1]
    enc_at = 2 * width
    edge_at = enc_at + freq_ref.shape[1]
    trow = target_ref[pl.ds(b, 1), :]
    erow = time_ref[pl.ds(b, 1), :]
    stacked = jnp.concatenate(
        [trow.astype(F32), erow.astype(F32), jnp.zeros((LANES - 2, events), F32)], axis=0
    )
    cols = stacked.T
    sub = lax.broadcasted_iota(I32, (events, events), 0)
    lane = lax.broadcasted_iota(I32, (events, events), 1)
    node_lane = lax.broadcasted_iota(I32, (events, node_dev), 1)
    tcol = cols[:, 0:1].astype(I32)
    ecol = cols[:, 1:2]
    seen = jnp.max(
        jnp.where(tcol == node_lane, node_time_ref[...].astype(F32), 0.0), axis=1, keepdims=True
    )
    for before in range(batches - 1):
        row = target_ref[before : before + 1, :]
        row = jnp.where((row < 0) | (before >= b), -2, row)
        seen = jnp.maximum(
            seen,
            jnp.max(
                jnp.where(tcol == row, time_ref[before : before + 1, :].astype(F32), 0.0),
                axis=1,
                keepdims=True,
            ),
        )
    angle = (ecol - seen) * freq_ref[...] + phase_ref[...]
    encoded = cosine(angle).astype(BF16)
    base_ref[...] = dot(encoded, w_ref[enc_at:edge_at, :]) + dot(edge_ref[0], w_ref[edge_at:, :])
    gcode_ref[...] = lane_code(tcol, events)
    same = (tcol == trow) & (trow >= 0)
    samef = same.astype(F32)
    same_ref[...] = samef.astype(BF16)
    earlier = jnp.max(jnp.where(sub < lane, samef, 0.0), axis=0, keepdims=True)
    first = jnp.where(earlier > 0.0, -1, trow)
    sub128 = lax.broadcasted_iota(I32, (LANES, events), 0)
    scode_ref[...] = jnp.where(
        (first & (LANES - 1)) == sub128, (first >> 7).astype(F32), -1.0
    ).astype(BF16)


def serve_rows(table_ref, code_ref, out_refs, step):
    blocks = table_ref.shape[0] // LANES
    table = table_ref[...]
    rows = out_refs[0].shape[0]
    for start in range(0, code_ref.shape[0], step):
        picked = dot(expand(code_ref[start : start + step, :], 0, blocks), table).astype(BF16)
        for part in range(0, step, rows):
            out_refs[(start + part) // rows][...] = picked[part : part + rows]


def serve_kernel(table_ref, own_code_ref, far_code_ref, own_ref, *far_refs):
    serve_rows(table_ref, own_code_ref, [own_ref.at[i : i + 256] for i in range(0, own_ref.shape[0], 256)], 256)
    serve_rows(table_ref, far_code_ref, far_refs, 512)


def local_kernel(table_ref, gcode_ref, base_ref, w_ref, out_ref):
    blocks = table_ref.shape[0] // LANES
    width = table_ref.shape[1]
    mem = dot(expand(gcode_ref[...], 0, blocks), table_ref[...])
    out_ref[:, :width] = base_ref[...] + dot(mem.astype(BF16), w_ref[:width, :])
    out_ref[:, width:] = mem


def update_kernel(
    last,
    at_ref,
    table_ref,
    back_ref,
    pcode_ref,
    local_ref,
    same_ref,
    scode_ref,
    w_ref,
    w_input_ref,
    w_hidden_ref,
    bias_input_ref,
    bias_hidden_ref,
    own_code_ref,
    far_code_ref,
    new_ref,
    own_out_ref,
    *far_out_refs,
):
    width = table_ref.shape[1]
    mem = local_ref[:, width:]
    hidden = dot(mem.astype(BF16), w_hidden_ref[...]) + bias_hidden_ref[...]
    source = dot(expand(pcode_ref[0], 0, back_ref.shape[0] // LANES), back_ref[...])
    w_source = w_ref[width : 2 * width, :]
    message = (local_ref[:, :width] + dot(source.astype(BF16), w_source)).astype(BF16)
    same = same_ref[...]
    total = dot(same, message)
    count = jnp.maximum(dot(same, jnp.ones((same.shape[0], LANES), BF16))[:, :1], 1.0)
    averaged = (total / count).astype(BF16)
    gates = dot(averaged, w_input_ref[...]) + bias_input_ref[...]
    reset = jax.nn.sigmoid(gates[:, :width] + hidden[:, :width])
    update = jax.nn.sigmoid(gates[:, width : 2 * width] + hidden[:, width : 2 * width])
    candidate = jnp.tanh(gates[:, 2 * width :] + reset * hidden[:, 2 * width :])
    fresh = ((1.0 - update) * candidate + update * mem).astype(BF16)
    ones = jnp.ones((fresh.shape[0], LANES), BF16)
    placed = jnp.concatenate([fresh, ones], axis=1)
    scode = scode_ref[...]
    one = jnp.ones((), BF16)
    zero = jnp.zeros((), BF16)
    blocks = table_ref.shape[0] // LANES
    group = 4
    for k in range(0, blocks, group):
        spread = jnp.concatenate(
            [jnp.where(scode == jnp.asarray(k + j, BF16), one, zero) for j in range(group)], axis=0
        )
        moved = dot(spread, placed)
        rows = slice(k * LANES, (k + group) * LANES)
        new_ref[rows, :] = jnp.where(
            moved[:, width : width + 1] > 0.0, moved[:, :width], table_ref[rows, :].astype(F32)
        ).astype(BF16)

    @pl.when(at_ref[0] < last)
    def _():
        serve_kernel(new_ref, own_code_ref, far_code_ref, own_out_ref, *far_out_refs)


def from_owner(own_rows, far_rows, owner, cap, turn):
    rows, _, width = own_rows.shape
    ys = len(far_rows) // 2

    def branch(root):
        y, z = root // 2, root % 2

        def body(own_rows, *far_rows):
            me = lax.axis_index("dom")
            my_y, my_z = me >> 1, me & 1

            def spread(which):
                part = far_rows[2 * y + which]
                moved = []
                for shift in range(1, ys):
                    there = (y + shift) % ys
                    pairs = [(2 * y + side, 2 * there + side) for side in range(2)]
                    block = lax.ppermute(far_rows[2 * there + which], "dom", pairs)
                    moved.append((there, block))
                for there, block in moved:
                    part = jnp.where(my_y == there, block, part)
                return part

            across = lax.ppermute(
                spread(1 - z),
                ("dom", "row"),
                [
                    ((2 * i + z) * rows + r, (2 * i + 1 - z) * rows + (r ^ turn))
                    for i in range(ys)
                    for r in range(rows)
                ],
            )
            mine = jnp.where(my_z == z, spread(z), across)
            return own_rows.at[:, cap:, :].set(mine.reshape(rows, -1, width))

        return body

    return lax.switch(owner, [branch(r) for r in range(2 * ys)], own_rows, *far_rows)


def shards(
    memory,
    node_time,
    target,
    source,
    event_time,
    edge_feat,
    owner_group,
    w_message,
    frequency,
    phase_shift,
    w_input,
    w_hidden,
    bias_input,
    bias_hidden,
):
    node_dev, width = memory.shape
    batches, events = target.shape
    rows = lax.axis_size("row")
    groups = lax.axis_size("dom")
    cap = 3 * events // (2 * rows)
    ocap = events // (2 * rows)
    per = cap + ocap
    shape = jax.ShapeDtypeStruct
    code = shape((events, LANES), BF16)

    me = lax.axis_index("dom").astype(I32)
    turn = rows - rows // 4
    flip = jnp.where((owner_group & 1) == (me & 1), 0, turn).astype(I32)
    ids, pcode = call(
        functools.partial(plan_kernel, cap, ocap, node_dev),
        (shape((groups, rows, batches * per), I32), shape((batches, events, LANES), BF16)),
        (source,),
        name="plan",
        scalars=(flip,),
    )
    asked = lax.all_to_all(
        ids.reshape(groups * rows, 1, batches * per), ("dom", "row"), 0, 0, tiled=True
    ).reshape(groups, rows, batches * per)
    times_row = node_time.reshape(1, node_dev)
    freq_row = frequency.reshape(1, -1)
    phase_row = phase_shift.reshape(1, -1)
    input_row = bias_input.reshape(1, -1)
    hidden_row = bias_hidden.reshape(1, -1)
    anywhere = pl.BlockSpec(memory_space=pl.ANY)

    def codes(b, after):
        return call(
            functools.partial(code_kernel, cap, per),
            (
                shape((rows * per, LANES), BF16),
                shape((groups * rows * ocap, LANES), BF16),
            ),
            (asked, after),
            flops=2 * 10**9,
            name="codes",
            specs={1: anywhere},
            scalars=(jnp.stack([b, me]),),
        )

    own_shape = shape((rows * per, width), BF16)
    far_shape = (shape((rows * ocap, width), BF16),) * groups
    own_rows, *far_rows = call(
        serve_kernel,
        (own_shape,) + far_shape,
        (memory,) + tuple(codes(jnp.zeros((), I32), asked)),
        flops=4 * 10**9,
        name="serve",
    )

    def batch(b, carry):
        table, own_rows, *far_rows = carry
        at = b.reshape(1)
        sent = from_owner(
            own_rows.reshape(rows, per, width),
            far_rows,
            lax.dynamic_index_in_dim(owner_group, b, 0, keepdims=False),
            cap,
            turn,
        )
        back = lax.all_to_all(sent, "row", 0, 0, tiled=True).reshape(rows * per, width)
        base, gcode, scode, same = call(
            functools.partial(prep_kernel, width),
            (
                shape((events, width), F32),
                code,
                shape((LANES, events), BF16),
                shape((events, events), BF16),
            ),
            (target, event_time, times_row, edge_feat, freq_row, phase_row, w_message, sent),
            flops=3 * 10**9,
            name="prep",
            specs={
                3: pl.BlockSpec((1,) + edge_feat.shape[1:], lambda i, at: (at[0], 0, 0)),
                7: anywhere,
            },
            scalars=(at,),
        )
        local = call(
            local_kernel,
            shape((events, 2 * width), F32),
            (table, gcode, base, w_message),
            flops=3 * 10**9,
            name="local",
        )
        own_code, far_code = codes(b + 1, sent)
        return call(
            functools.partial(update_kernel, batches - 1),
            (shape((node_dev, width), BF16), own_shape) + far_shape,
            (
                table,
                back,
                pcode,
                local,
                same,
                scode,
                w_message,
                w_input,
                w_hidden,
                input_row,
                hidden_row,
                own_code,
                far_code,
            ),
            flops=6 * 10**9,
            name="update",
            specs={2: pl.BlockSpec((1, events, LANES), lambda i, at: (at[0], 0, 0))},
            scalars=(at,),
        )

    return lax.fori_loop(0, batches, batch, (memory, own_rows, *far_rows))[0]


def solution(mesh):
    in_specs = (
        P(("dom", "row"), None),
        P(("dom", "row")),
        P(None, ("dom", "row")),
        P(None, ("dom", "row")),
        P(None, ("dom", "row")),
        P(None, ("dom", "row"), None),
        P(),
        P(),
        P(),
        P(),
        P(),
        P(),
        P(),
        P(),
    )
    out_specs = P(("dom", "row"), None)
    return jax.shard_map(shards, mesh=mesh, in_specs=in_specs, out_specs=out_specs, check_vma=False)
```

```python
import functools

import jax
import jax.numpy as jnp
from jax import lax
from jax.experimental import pallas as pl
from jax.experimental.pallas import tpu as pltpu
from jax.sharding import PartitionSpec as P

LANES = 128
F32 = jnp.float32
BF16 = jnp.bfloat16
I32 = jnp.int32
MIB = 1024 * 1024
VMEM_MIB = dict(plan=6, stage=6, codes=6, prep=12, serve=8, update=16)


def whole():
    return pl.BlockSpec(memory_space=pltpu.VMEM)


def call(kernel, out_shape, args, flops=0, name=None, specs=None, scalars=()):
    moved = sum(a.size * a.dtype.itemsize for a in args)
    moved += sum(o.size * o.dtype.itemsize for o in jax.tree.leaves(out_shape))
    specs = specs or {}
    return pl.pallas_call(
        kernel,
        out_shape=out_shape,
        grid_spec=pltpu.PrefetchScalarGridSpec(
            num_scalar_prefetch=len(scalars),
            grid=(1,) if scalars else (),
            in_specs=[specs.get(i, whole()) for i in range(len(args))],
            out_specs=jax.tree.map(lambda _: whole(), out_shape),
        ),
        compiler_params=pltpu.CompilerParams(vmem_limit_bytes=VMEM_MIB[name] * MIB),
        cost_estimate=pl.CostEstimate(flops=flops, bytes_accessed=moved, transcendentals=0),
        name=name,
    )(*scalars, *args)


def dot(a, b):
    return jnp.dot(a, b, preferred_element_type=F32)


def dot_nt(a, b):
    return lax.dot_general(a, b, (((1,), (1,)), ((), ())), preferred_element_type=F32)


def lane_code_f32(index_col, rows):
    lane = lax.broadcasted_iota(I32, (rows, LANES), 1)
    hit = (index_col & (LANES - 1)) == lane
    return jnp.where(hit, (index_col >> 7).astype(F32), -1.0)


def lane_code(index_col, rows):
    return lane_code_f32(index_col, rows).astype(BF16)


def expand(code, first, count):
    one = jnp.ones((), BF16)
    zero = jnp.zeros((), BF16)
    return jnp.concatenate(
        [jnp.where(code == jnp.asarray(k, BF16), one, zero) for k in range(first, first + count)],
        axis=1,
    )


def stage_kernel(_, *refs):
    count = len(refs) // 2
    for given, kept in zip(refs[:count], refs[count:]):
        kept[...] = given[...]


def plan_kernel(cap, ocap, node_dev, flip_ref, source_ref, ids_ref, pcode_ref):
    batches, events = source_ref.shape
    rows = ids_ref.shape[1]
    per = cap + ocap
    own_total = rows * cap
    group_nodes = rows * node_dev
    upper = (
        lax.broadcasted_iota(I32, (events, events), 0)
        <= lax.broadcasted_iota(I32, (events, events), 1)
    ).astype(F32).astype(BF16)
    bucket_iota = lax.broadcasted_iota(I32, (2 * rows, events), 0)
    lane_iota = lax.broadcasted_iota(I32, (LANES, events), 0)
    high = jnp.zeros((rows, LANES), F32)
    low = jnp.zeros((rows, LANES), F32)
    places = []
    for b in range(batches):
        src = source_ref[b : b + 1, :]
        far = src >= group_nodes
        local = jnp.where(far, src - group_nodes, src)
        dest = local // node_dev
        offset = local - dest * node_dev
        bucket = jnp.where(far, dest + rows, dest)
        hit = bucket == bucket_iota
        hitf = hit.astype(F32)
        running = dot(hitf.astype(BF16), upper)
        rank = jnp.sum(hitf * running, axis=0, keepdims=True).astype(I32) - 1
        slot = jnp.where(far, rank + cap, rank)
        both = (hitf[:rows] + hitf[rows:]).astype(BF16)
        spot = (slot + b * per == lane_iota).astype(F32)
        high = high + dot_nt(both, (spot * (offset >> 6).astype(F32)).astype(BF16))
        low = low + dot_nt(both, (spot * (offset & 63).astype(F32)).astype(BF16))
        places.append(
            jnp.where(far, own_total + (dest ^ flip_ref[b]) * ocap + rank, dest * cap + rank)
        )
    ids = high.astype(I32) * 64 + low.astype(I32)
    for g in range(ids_ref.shape[0]):
        ids_ref[g] = ids
    stacked = jnp.concatenate(
        [p.astype(F32) for p in places] + [jnp.zeros((LANES - batches, events), F32)], axis=0
    )
    cols = stacked.T
    for b in range(batches):
        pcode_ref[b] = lane_code(cols[:, b : b + 1].astype(I32), events)


def spread_codes(ids, first, count):
    rows = ids.shape[0]
    total = rows * count
    place = lax.broadcasted_iota(I32, (total, LANES), 0)
    lane = lax.broadcasted_iota(I32, (total, LANES), 1)
    row = place // count
    copy = (row[:, :rows] == lane[:, :rows]).astype(F32).astype(BF16)
    keep = (lane == first + place - row * count).astype(F32)
    ones = jnp.ones((LANES, LANES), BF16)

    def everywhere(part):
        taken = dot(copy, part.astype(F32).astype(BF16)) * keep
        return dot(taken.astype(BF16), ones)

    low = everywhere(ids & (LANES - 1))
    high = everywhere(ids >> 7)
    return jnp.where(low == lane.astype(F32), high, -1.0).astype(BF16)


def code_kernel(cap, per, at_ref, asked_ref, _, own_ref, far_ref):
    b = at_ref[0]
    groups, rows, _ = asked_ref.shape
    own_ref[...] = spread_codes(asked_ref[at_ref[1]], b * per, cap)
    block = rows * (per - cap)
    for g in range(groups):
        far_ref[g * block : (g + 1) * block, :] = spread_codes(
            asked_ref[g], b * per + cap, per - cap
        )


def cosine(x):
    turns = jnp.floor(x * 0.15915494309189535 + 0.5)
    r = (x - turns * 6.28125) - turns * 0.0019353071795864769
    z = r * r
    value = jnp.full_like(z, 1.0 / 20922789888000.0)
    for factor in (
        -1.0 / 87178291200.0,
        1.0 / 479001600.0,
        -1.0 / 3628800.0,
        1.0 / 40320.0,
        -1.0 / 720.0,
        1.0 / 24.0,
        -0.5,
        1.0,
    ):
        value = value * z + factor
    return value


def prep_kernel(
    width,
    at_ref,
    table_ref,
    target_ref,
    time_ref,
    node_time_ref,
    edge_ref,
    freq_ref,
    phase_ref,
    w_ref,
    _,
    local_ref,
    scode_ref,
    same_ref,
):
    b = at_ref[0]
    batches, events = target_ref.shape
    node_dev = node_time_ref.shape[1]
    enc_at = 2 * width
    edge_at = enc_at + freq_ref.shape[1]
    trow = target_ref[pl.ds(b, 1), :]
    erow = time_ref[pl.ds(b, 1), :]
    stacked = jnp.concatenate(
        [trow.astype(F32), erow.astype(F32), jnp.zeros((LANES - 2, events), F32)], axis=0
    )
    cols = stacked.T
    sub = lax.broadcasted_iota(I32, (events, events), 0)
    lane = lax.broadcasted_iota(I32, (events, events), 1)
    node_lane = lax.broadcasted_iota(I32, (events, node_dev), 1)
    tcol = cols[:, 0:1].astype(I32)
    ecol = cols[:, 1:2]
    seen = jnp.max(
        jnp.where(tcol == node_lane, node_time_ref[...].astype(F32), 0.0), axis=1, keepdims=True
    )
    for before in range(batches - 1):
        row = target_ref[before : before + 1, :]
        row = jnp.where((row < 0) | (before >= b), -2, row)
        seen = jnp.maximum(
            seen,
            jnp.max(
                jnp.where(tcol == row, time_ref[before : before + 1, :].astype(F32), 0.0),
                axis=1,
                keepdims=True,
            ),
        )
    angle = (ecol - seen) * freq_ref[...] + phase_ref[...]
    encoded = cosine(angle).astype(BF16)
    mem = dot(expand(lane_code(tcol, events), 0, node_dev // LANES), table_ref[...])
    local_ref[:, :width] = (
        dot(encoded, w_ref[enc_at:edge_at, :])
        + dot(edge_ref[0], w_ref[edge_at:, :])
        + dot(mem.astype(BF16), w_ref[:width, :])
    )
    local_ref[:, width:] = mem
    same = (tcol == trow) & (trow >= 0)
    samef = same.astype(F32)
    same_ref[...] = samef.astype(BF16)
    earlier = jnp.max(jnp.where(sub < lane, samef, 0.0), axis=0, keepdims=True)
    first = jnp.where(earlier > 0.0, -1, trow)
    sub128 = lax.broadcasted_iota(I32, (LANES, events), 0)
    scode_ref[...] = jnp.where(
        (first & (LANES - 1)) == sub128, (first >> 7).astype(F32), -1.0
    ).astype(BF16)


def serve_rows(table_ref, code_ref, out_refs, step):
    blocks = table_ref.shape[0] // LANES
    table = table_ref[...]
    rows = out_refs[0].shape[0]
    for start in range(0, code_ref.shape[0], step):
        picked = dot(expand(code_ref[start : start + step, :], 0, blocks), table).astype(BF16)
        for part in range(0, step, rows):
            out_refs[(start + part) // rows][...] = picked[part : part + rows]


def serve_kernel(table_ref, own_code_ref, far_code_ref, own_ref, *far_refs):
    serve_rows(table_ref, own_code_ref, [own_ref.at[i : i + 256] for i in range(0, own_ref.shape[0], 256)], 256)
    serve_rows(table_ref, far_code_ref, far_refs, 512)


def update_kernel(
    last,
    at_ref,
    table_ref,
    own_back_ref,
    far_back_ref,
    pcode_ref,
    local_ref,
    same_ref,
    scode_ref,
    w_ref,
    w_input_ref,
    w_hidden_ref,
    bias_input_ref,
    bias_hidden_ref,
    own_code_ref,
    far_code_ref,
    new_ref,
    own_out_ref,
    *far_out_refs,
):
    width = table_ref.shape[1]
    mem = local_ref[:, width:]
    hidden = dot(mem.astype(BF16), w_hidden_ref[...]) + bias_hidden_ref[...]
    own_blocks = own_back_ref.shape[0] // LANES
    far_blocks = far_back_ref.shape[0] // LANES
    pcode = pcode_ref[0]
    source = dot(expand(pcode, 0, own_blocks), own_back_ref[...]) + dot(
        expand(pcode, own_blocks, far_blocks), far_back_ref[...]
    )
    w_source = w_ref[width : 2 * width, :]
    message = (local_ref[:, :width] + dot(source.astype(BF16), w_source)).astype(BF16)
    same = same_ref[...]
    total = dot(same, message)
    count = jnp.maximum(dot(same, jnp.ones((same.shape[0], LANES), BF16))[:, :1], 1.0)
    averaged = (total / count).astype(BF16)
    gates = dot(averaged, w_input_ref[...]) + bias_input_ref[...]
    reset = jax.nn.sigmoid(gates[:, :width] + hidden[:, :width])
    update = jax.nn.sigmoid(gates[:, width : 2 * width] + hidden[:, width : 2 * width])
    candidate = jnp.tanh(gates[:, 2 * width :] + reset * hidden[:, 2 * width :])
    fresh = ((1.0 - update) * candidate + update * mem).astype(BF16)
    ones = jnp.ones((fresh.shape[0], LANES), BF16)
    placed = jnp.concatenate([fresh, ones], axis=1)
    scode = scode_ref[...]
    one = jnp.ones((), BF16)
    zero = jnp.zeros((), BF16)
    blocks = table_ref.shape[0] // LANES
    group = 4
    for k in range(0, blocks, group):
        spread = jnp.concatenate(
            [jnp.where(scode == jnp.asarray(k + j, BF16), one, zero) for j in range(group)], axis=0
        )
        moved = dot(spread, placed)
        rows = slice(k * LANES, (k + group) * LANES)
        new_ref[rows, :] = jnp.where(
            moved[:, width : width + 1] > 0.0, moved[:, :width], table_ref[rows, :].astype(F32)
        ).astype(BF16)

    @pl.when(at_ref[0] < last)
    def _():
        serve_kernel(new_ref, own_code_ref, far_code_ref, own_out_ref, *far_out_refs)


def fetch(own_rows, far_rows, owner, turn):
    rows = own_rows.shape[0]
    ys = len(far_rows) // 2

    def branch(root):
        y, z = root // 2, root % 2

        def body(own_rows, *far_rows):
            me = lax.axis_index("dom")
            my_y, my_z = me >> 1, me & 1

            def spread(which):
                part = far_rows[2 * y + which]
                moved = []
                for shift in range(1, ys):
                    there = (y + shift) % ys
                    pairs = [(2 * y + side, 2 * there + side) for side in range(2)]
                    block = lax.ppermute(far_rows[2 * there + which], "dom", pairs)
                    moved.append((there, block))
                for there, block in moved:
                    part = jnp.where(my_y == there, block, part)
                return part

            across = lax.ppermute(
                spread(1 - z),
                ("dom", "row"),
                [
                    ((2 * i + z) * rows + r, (2 * i + 1 - z) * rows + (r ^ turn))
                    for i in range(ys)
                    for r in range(rows)
                ],
            )
            along = spread(z)
            own_back = lax.all_to_all(own_rows, "row", 0, 0, tiled=True)
            seat = my_z + (own_back[0, 0, 0].astype(F32) * 0.0).astype(I32)
            return own_back, jnp.where(seat == z, along, across)

        return body

    return lax.switch(owner, [branch(r) for r in range(2 * ys)], own_rows, *far_rows)


def shards(
    memory,
    node_time,
    target,
    source,
    event_time,
    edge_feat,
    owner_group,
    w_message,
    frequency,
    phase_shift,
    w_input,
    w_hidden,
    bias_input,
    bias_hidden,
):
    node_dev, width = memory.shape
    batches, events = target.shape
    rows = lax.axis_size("row")
    groups = lax.axis_size("dom")
    cap = 3 * events // (2 * rows)
    ocap = events // (2 * rows)
    per = cap + ocap
    shape = jax.ShapeDtypeStruct
    me = lax.axis_index("dom").astype(I32)
    turn = rows - rows // 4
    flip = jnp.where((owner_group & 1) == (me & 1), 0, turn).astype(I32)
    row_vectors = (
        node_time.reshape(1, node_dev),
        frequency.reshape(1, -1),
        phase_shift.reshape(1, -1),
        bias_input.reshape(1, -1),
        bias_hidden.reshape(1, -1),
    )
    anywhere = pl.BlockSpec(memory_space=pl.ANY)
    ids, pcode = call(
        functools.partial(plan_kernel, cap, ocap, node_dev),
        (
            shape((groups, rows, batches * per), I32),
            shape((batches, events, LANES), BF16),
        ),
        (source,),
        name="plan",
        scalars=(flip,),
    )
    given = (memory,) + row_vectors
    table, times_row, freq_row, phase_row, input_row, hidden_row = call(
        stage_kernel,
        tuple(shape(v.shape, v.dtype) for v in given),
        (ids,) + given,
        flops=2 * 10**9,
        name="stage",
        specs={0: anywhere},
    )
    asked = lax.all_to_all(
        ids.reshape(groups * rows, 1, batches * per), ("dom", "row"), 0, 0, tiled=True
    ).reshape(groups, rows, batches * per)
    def codes(b, after):
        return call(
            functools.partial(code_kernel, cap, per),
            (
                shape((rows * cap, LANES), BF16),
                shape((groups * rows * ocap, LANES), BF16),
            ),
            (asked, after),
            flops=2 * 10**9,
            name="codes",
            specs={1: anywhere},
            scalars=(jnp.stack([b, me]),),
        )

    own_shape = shape((rows * cap, width), BF16)
    far_shape = (shape((rows * ocap, width), BF16),) * groups
    own_rows, *far_rows = call(
        serve_kernel,
        (own_shape,) + far_shape,
        (table,) + tuple(codes(jnp.zeros((), I32), asked)),
        flops=4 * 10**9,
        name="serve",
    )

    def batch(b, carry):
        table, own_rows, *far_rows = carry
        at = b.reshape(1)
        own_back, mine = fetch(
            own_rows.reshape(rows, cap, width),
            far_rows,
            lax.dynamic_index_in_dim(owner_group, b, 0, keepdims=False),
            turn,
        )
        far_back = lax.all_to_all(mine.reshape(rows, ocap, width), "row", 0, 0, tiled=True)
        local, scode, same = call(
            functools.partial(prep_kernel, width),
            (
                shape((events, 2 * width), F32),
                shape((LANES, events), BF16),
                shape((events, events), BF16),
            ),
            (table, target, event_time, times_row, edge_feat, freq_row, phase_row, w_message, mine),
            flops=5 * 10**9,
            name="prep",
            specs={
                4: pl.BlockSpec((1,) + edge_feat.shape[1:], lambda i, at: (at[0], 0, 0)),
                8: anywhere,
            },
            scalars=(at,),
        )
        own_code, far_code = codes(b + 1, mine)
        return call(
            functools.partial(update_kernel, batches - 1),
            (shape((node_dev, width), BF16), own_shape) + far_shape,
            (
                table,
                own_back.reshape(rows * cap, width),
                far_back.reshape(rows * ocap, width),
                pcode,
                local,
                same,
                scode,
                w_message,
                w_input,
                w_hidden,
                input_row,
                hidden_row,
                own_code,
                far_code,
            ),
            flops=6 * 10**9,
            name="update",
            specs={3: pl.BlockSpec((1, events, LANES), lambda i, at: (at[0], 0, 0))},
            scalars=(at,),
        )

    return lax.fori_loop(0, batches, batch, (table, own_rows, *far_rows))[0]


def solution(mesh):
    in_specs = (
        P(("dom", "row"), None),
        P(("dom", "row")),
        P(None, ("dom", "row")),
        P(None, ("dom", "row")),
        P(None, ("dom", "row")),
        P(None, ("dom", "row"), None),
        P(),
        P(),
        P(),
        P(),
        P(),
        P(),
        P(),
        P(),
    )
    out_specs = P(("dom", "row"), None)
    return jax.shard_map(shards, mesh=mesh, in_specs=in_specs, out_specs=out_specs, check_vma=False)
```

```python
import functools

import jax
import jax.numpy as jnp
from jax import lax
from jax.experimental import pallas as pl
from jax.experimental.pallas import tpu as pltpu
from jax.sharding import PartitionSpec as P

LANES = 128
F32 = jnp.float32
BF16 = jnp.bfloat16
I32 = jnp.int32
MIB = 1024 * 1024
VMEM_MIB = dict(plan=6, stage=6, codes=6, prep=16, serve=8, update=16)


def whole():
    return pl.BlockSpec(memory_space=pltpu.VMEM)


def call(kernel, out_shape, args, flops=0, name=None, specs=None, scalars=(), aliases=None):
    moved = sum(a.size * a.dtype.itemsize for a in args)
    moved += sum(o.size * o.dtype.itemsize for o in jax.tree.leaves(out_shape))
    specs = specs or {}
    return pl.pallas_call(
        kernel,
        out_shape=out_shape,
        grid_spec=pltpu.PrefetchScalarGridSpec(
            num_scalar_prefetch=len(scalars),
            grid=(1,) if scalars else (),
            in_specs=[specs.get(i, whole()) for i in range(len(args))],
            out_specs=jax.tree.map(lambda _: whole(), out_shape),
        ),
        input_output_aliases=aliases or {},
        compiler_params=pltpu.CompilerParams(vmem_limit_bytes=VMEM_MIB[name] * MIB),
        cost_estimate=pl.CostEstimate(flops=flops, bytes_accessed=moved, transcendentals=0),
        name=name,
    )(*scalars, *args)


def dot(a, b):
    return jnp.dot(a, b, preferred_element_type=F32)


def dot_nt(a, b):
    return lax.dot_general(a, b, (((1,), (1,)), ((), ())), preferred_element_type=F32)


def lane_code_f32(index_col, rows):
    lane = lax.broadcasted_iota(I32, (rows, LANES), 1)
    hit = (index_col & (LANES - 1)) == lane
    return jnp.where(hit, (index_col >> 7).astype(F32), -1.0)


def lane_code(index_col, rows):
    return lane_code_f32(index_col, rows).astype(BF16)


def expand(code, first, count):
    one = jnp.ones((), BF16)
    zero = jnp.zeros((), BF16)
    return jnp.concatenate(
        [jnp.where(code == jnp.asarray(k, BF16), one, zero) for k in range(first, first + count)],
        axis=1,
    )


def stage_kernel(_, *refs):
    count = len(refs) // 2
    for given, kept in zip(refs[:count], refs[count:]):
        kept[...] = given[...]


def plan_kernel(cap, ocap, node_dev, flip_ref, source_ref, ids_ref, pcode_ref):
    batches, events = source_ref.shape
    rows = ids_ref.shape[1]
    per = cap + ocap
    group_nodes = rows * node_dev
    upper = (
        lax.broadcasted_iota(I32, (events, events), 0)
        <= lax.broadcasted_iota(I32, (events, events), 1)
    ).astype(F32).astype(BF16)
    bucket_iota = lax.broadcasted_iota(I32, (2 * rows, events), 0)
    lane_iota = lax.broadcasted_iota(I32, (LANES, events), 0)
    high = jnp.zeros((rows, LANES), F32)
    low = jnp.zeros((rows, LANES), F32)
    places = []
    for b in range(batches):
        src = source_ref[b : b + 1, :]
        far = src >= group_nodes
        local = jnp.where(far, src - group_nodes, src)
        dest = local // node_dev
        offset = local - dest * node_dev
        bucket = jnp.where(far, dest + rows, dest)
        hit = bucket == bucket_iota
        hitf = hit.astype(F32)
        running = dot(hitf.astype(BF16), upper)
        rank = jnp.sum(hitf * running, axis=0, keepdims=True).astype(I32) - 1
        slot = jnp.where(far, rank + cap, rank)
        both = (hitf[:rows] + hitf[rows:]).astype(BF16)
        spot = (slot + b * per == lane_iota).astype(F32)
        high = high + dot_nt(both, (spot * (offset >> 6).astype(F32)).astype(BF16))
        low = low + dot_nt(both, (spot * (offset & 63).astype(F32)).astype(BF16))
        places.append(jnp.where(far, dest ^ flip_ref[b], dest) * per + slot)
    ids = high.astype(I32) * 64 + low.astype(I32)
    for g in range(ids_ref.shape[0]):
        ids_ref[g] = ids
    stacked = jnp.concatenate(
        [p.astype(F32) for p in places] + [jnp.zeros((LANES - batches, events), F32)], axis=0
    )
    cols = stacked.T
    for b in range(batches):
        pcode_ref[b] = lane_code(cols[:, b : b + 1].astype(I32), events)


def spread_codes(ids, first, count):
    rows = ids.shape[0]
    total = rows * count
    place = lax.broadcasted_iota(I32, (total, LANES), 0)
    lane = lax.broadcasted_iota(I32, (total, LANES), 1)
    row = place // count
    copy = (row[:, :rows] == lane[:, :rows]).astype(F32).astype(BF16)
    keep = (lane == first + place - row * count).astype(F32)
    ones = jnp.ones((LANES, LANES), BF16)

    def everywhere(part):
        taken = dot(copy, part.astype(F32).astype(BF16)) * keep
        return dot(taken.astype(BF16), ones)

    low = everywhere(ids & (LANES - 1))
    high = everywhere(ids >> 7)
    return jnp.where(low == lane.astype(F32), high, -1.0).astype(BF16)


def write_codes(b, me, cap, per, asked_ref, own_ref, far_ref):
    groups, rows, _ = asked_ref.shape
    own_ref[...] = spread_codes(asked_ref[me], b * per, per)
    block = rows * (per - cap)
    for g in range(groups):
        far_ref[g * block : (g + 1) * block, :] = spread_codes(
            asked_ref[g], b * per + cap, per - cap
        )


def code_kernel(cap, per, at_ref, asked_ref, own_ref, far_ref):
    write_codes(at_ref[0], at_ref[1], cap, per, asked_ref, own_ref, far_ref)


def cosine(x):
    turns = jnp.floor(x * 0.15915494309189535 + 0.5)
    r = (x - turns * 6.28125) - turns * 0.0019353071795864769
    z = r * r
    value = jnp.full_like(z, 1.0 / 20922789888000.0)
    for factor in (
        -1.0 / 87178291200.0,
        1.0 / 479001600.0,
        -1.0 / 3628800.0,
        1.0 / 40320.0,
        -1.0 / 720.0,
        1.0 / 24.0,
        -0.5,
        1.0,
    ):
        value = value * z + factor
    return value


def prep_kernel(
    width,
    cap,
    per,
    at_ref,
    table_ref,
    target_ref,
    time_ref,
    node_time_ref,
    edge_ref,
    freq_ref,
    phase_ref,
    w_ref,
    asked_ref,
    _,
    local_ref,
    scode_ref,
    same_ref,
    own_code_ref,
    far_code_ref,
):
    b = at_ref[0]
    write_codes(b + 1, at_ref[1], cap, per, asked_ref, own_code_ref, far_code_ref)
    batches, events = target_ref.shape
    node_dev = node_time_ref.shape[1]
    enc_at = 2 * width
    edge_at = enc_at + freq_ref.shape[1]
    trow = target_ref[pl.ds(b, 1), :]
    erow = time_ref[pl.ds(b, 1), :]
    stacked = jnp.concatenate(
        [trow.astype(F32), erow.astype(F32), jnp.zeros((LANES - 2, events), F32)], axis=0
    )
    cols = stacked.T
    sub = lax.broadcasted_iota(I32, (events, events), 0)
    lane = lax.broadcasted_iota(I32, (events, events), 1)
    node_lane = lax.broadcasted_iota(I32, (events, node_dev), 1)
    tcol = cols[:, 0:1].astype(I32)
    ecol = cols[:, 1:2]
    seen = jnp.max(
        jnp.where(tcol == node_lane, node_time_ref[...].astype(F32), 0.0), axis=1, keepdims=True
    )
    for before in range(batches - 1):
        row = target_ref[before : before + 1, :]
        row = jnp.where((row < 0) | (before >= b), -2, row)
        seen = jnp.maximum(
            seen,
            jnp.max(
                jnp.where(tcol == row, time_ref[before : before + 1, :].astype(F32), 0.0),
                axis=1,
                keepdims=True,
            ),
        )
    angle = (ecol - seen) * freq_ref[...] + phase_ref[...]
    encoded = cosine(angle).astype(BF16)
    mem = dot(expand(lane_code(tcol, events), 0, node_dev // LANES), table_ref[...])
    local_ref[:, :width] = (
        dot(encoded, w_ref[enc_at:edge_at, :])
        + dot(edge_ref[0], w_ref[edge_at:, :])
        + dot(mem.astype(BF16), w_ref[:width, :])
    )
    local_ref[:, width:] = mem
    same = (tcol == trow) & (trow >= 0)
    samef = same.astype(F32)
    same_ref[...] = samef.astype(BF16)
    earlier = jnp.max(jnp.where(sub < lane, samef, 0.0), axis=0, keepdims=True)
    first = jnp.where(earlier > 0.0, -1, trow)
    sub128 = lax.broadcasted_iota(I32, (LANES, events), 0)
    scode_ref[...] = jnp.where(
        (first & (LANES - 1)) == sub128, (first >> 7).astype(F32), -1.0
    ).astype(BF16)


def serve_rows(table_ref, code_ref, out_refs, step):
    blocks = table_ref.shape[0] // LANES
    table = table_ref[...]
    rows = out_refs[0].shape[0]
    for start in range(0, code_ref.shape[0], step):
        picked = dot(expand(code_ref[start : start + step, :], 0, blocks), table).astype(BF16)
        for part in range(0, step, rows):
            out_refs[(start + part) // rows][...] = picked[part : part + rows]


def serve_own_kernel(table_ref, own_code_ref, own_ref):
    halves = [own_ref.at[i : i + 512] for i in range(0, own_ref.shape[0], 512)]
    serve_rows(table_ref, own_code_ref, halves, 512)


def serve_far_kernel(table_ref, far_code_ref, *far_refs):
    serve_rows(table_ref, far_code_ref, far_refs, 512)


def update_kernel(
    last,
    at_ref,
    table_ref,
    back_ref,
    pcode_ref,
    local_ref,
    same_ref,
    scode_ref,
    w_ref,
    w_input_ref,
    w_hidden_ref,
    bias_input_ref,
    bias_hidden_ref,
    far_code_ref,
    new_ref,
    *far_out_refs,
):
    width = table_ref.shape[1]
    mem = local_ref[:, width:]
    hidden = dot(mem.astype(BF16), w_hidden_ref[...]) + bias_hidden_ref[...]
    source = dot(expand(pcode_ref[0], 0, back_ref.shape[0] // LANES), back_ref[...])
    w_source = w_ref[width : 2 * width, :]
    message = (local_ref[:, :width] + dot(source.astype(BF16), w_source)).astype(BF16)
    same = same_ref[...]
    total = dot(same, message)
    count = jnp.maximum(dot(same, jnp.ones((same.shape[0], LANES), BF16))[:, :1], 1.0)
    averaged = (total / count).astype(BF16)
    gates = dot(averaged, w_input_ref[...]) + bias_input_ref[...]
    reset = jax.nn.sigmoid(gates[:, :width] + hidden[:, :width])
    update = jax.nn.sigmoid(gates[:, width : 2 * width] + hidden[:, width : 2 * width])
    candidate = jnp.tanh(gates[:, 2 * width :] + reset * hidden[:, 2 * width :])
    fresh = ((1.0 - update) * candidate + update * mem).astype(BF16)
    ones = jnp.ones((fresh.shape[0], LANES), BF16)
    placed = jnp.concatenate([fresh, ones], axis=1)
    scode = scode_ref[...]
    one = jnp.ones((), BF16)
    zero = jnp.zeros((), BF16)
    blocks = table_ref.shape[0] // LANES
    group = 4
    for k in range(0, blocks, group):
        spread = jnp.concatenate(
            [jnp.where(scode == jnp.asarray(k + j, BF16), one, zero) for j in range(group)], axis=0
        )
        moved = dot(spread, placed)
        rows = slice(k * LANES, (k + group) * LANES)
        new_ref[rows, :] = jnp.where(
            moved[:, width : width + 1] > 0.0, moved[:, :width], table_ref[rows, :].astype(F32)
        ).astype(BF16)

    @pl.when(at_ref[0] < last)
    def _():
        serve_far_kernel(new_ref, far_code_ref, *far_out_refs)


def collect(table, own_code, far_rows, owner, turn, rows):
    width = table.shape[1]
    ys = len(far_rows) // 2

    def branch(root):
        y, z = root // 2, root % 2

        def body(table, own_code, *far_rows):
            me = lax.axis_index("dom")
            my_y, my_z = me >> 1, me & 1

            def spread(which):
                part = far_rows[2 * y + which]
                moved = []
                for shift in range(1, ys):
                    there = (y + shift) % ys
                    pairs = [(2 * y + side, 2 * there + side) for side in range(2)]
                    block = lax.ppermute(far_rows[2 * there + which], "dom", pairs)
                    moved.append((there, block))
                for there, block in moved:
                    part = jnp.where(my_y == there, block, part)
                return part

            own_rows = call(
                serve_own_kernel,
                jax.ShapeDtypeStruct((own_code.shape[0], width), BF16),
                (table, own_code),
                flops=2 * 10**9,
                name="serve",
            ).reshape(rows, -1, width)
            across = lax.ppermute(
                spread(1 - z),
                ("dom", "row"),
                [
                    ((2 * i + z) * rows + r, (2 * i + 1 - z) * rows + (r ^ turn))
                    for i in range(ys)
                    for r in range(rows)
                ],
            )
            mine = jnp.where(my_z == z, spread(z), across).reshape(rows, -1, width)
            return own_rows.at[:, own_rows.shape[1] - mine.shape[1] :, :].set(mine)

        return body

    return lax.switch(owner, [branch(r) for r in range(2 * ys)], table, own_code, *far_rows)


def shards(
    memory,
    node_time,
    target,
    source,
    event_time,
    edge_feat,
    owner_group,
    w_message,
    frequency,
    phase_shift,
    w_input,
    w_hidden,
    bias_input,
    bias_hidden,
):
    node_dev, width = memory.shape
    batches, events = target.shape
    rows = lax.axis_size("row")
    groups = lax.axis_size("dom")
    cap = 3 * events // (2 * rows)
    ocap = events // (2 * rows)
    per = cap + ocap
    shape = jax.ShapeDtypeStruct
    me = lax.axis_index("dom").astype(I32)
    turn = rows - rows // 4
    flip = jnp.where((owner_group & 1) == (me & 1), 0, turn).astype(I32)
    row_vectors = (
        node_time.reshape(1, node_dev),
        frequency.reshape(1, -1),
        phase_shift.reshape(1, -1),
    )
    input_row = bias_input.reshape(1, -1)
    hidden_row = bias_hidden.reshape(1, -1)
    anywhere = pl.BlockSpec(memory_space=pl.ANY)
    ids, pcode = call(
        functools.partial(plan_kernel, cap, ocap, node_dev),
        (
            shape((groups, rows, batches * per), I32),
            shape((batches, events, LANES), BF16),
        ),
        (source,),
        name="plan",
        scalars=(flip,),
    )
    given = (memory,) + row_vectors
    table, times_row, freq_row, phase_row = call(
        stage_kernel,
        tuple(shape(v.shape, v.dtype) for v in given),
        (ids,) + given,
        flops=2 * 10**9,
        name="stage",
        specs={0: anywhere},
    )
    asked = lax.all_to_all(
        ids.reshape(groups * rows, 1, batches * per), ("dom", "row"), 0, 0, tiled=True
    ).reshape(groups, rows, batches * per)
    code_shapes = (
        shape((rows * per, LANES), BF16),
        shape((groups * rows * ocap, LANES), BF16),
    )
    own_code, far_code = call(
        functools.partial(code_kernel, cap, per),
        code_shapes,
        (asked,),
        flops=2 * 10**9,
        name="codes",
        scalars=(jnp.stack([jnp.zeros((), I32), me]),),
    )
    far_shape = (shape((rows * ocap, width), BF16),) * groups
    far_rows = call(
        serve_far_kernel, far_shape, (memory, far_code), flops=4 * 10**9, name="serve"
    )

    def batch(b, carry):
        table, own_code, *far_rows = carry
        at = jnp.stack([b, me])
        sent = collect(
            table,
            own_code,
            far_rows,
            lax.dynamic_index_in_dim(owner_group, b, 0, keepdims=False),
            turn,
            rows,
        )
        back = lax.all_to_all(sent, "row", 0, 0, tiled=True).reshape(rows * per, width)
        local, scode, same, next_own, next_far = call(
            functools.partial(prep_kernel, width, cap, per),
            (
                shape((events, 2 * width), F32),
                shape((LANES, events), BF16),
                shape((events, events), BF16),
            )
            + code_shapes,
            (table, target, event_time, times_row, edge_feat, freq_row, phase_row, w_message, asked, sent),
            flops=5 * 10**9,
            name="prep",
            specs={
                4: pl.BlockSpec((1,) + edge_feat.shape[1:], lambda i, at: (at[0], 0, 0)),
                9: anywhere,
            },
            scalars=(at,),
        )
        result = call(
            functools.partial(update_kernel, batches - 1),
            (shape((node_dev, width), BF16),) + far_shape,
            (
                table,
                back,
                pcode,
                local,
                same,
                scode,
                w_message,
                w_input,
                w_hidden,
                input_row,
                hidden_row,
                next_far,
            ),
            flops=6 * 10**9,
            name="update",
            specs={2: pl.BlockSpec((1, events, LANES), lambda i, at: (at[0], 0, 0))},
            scalars=(at,),
            aliases={1: 0},
        )
        return (result[0], next_own) + tuple(result[1:])

    return lax.fori_loop(0, batches, batch, (table, own_code, *far_rows))[0]


def solution(mesh):
    in_specs = (
        P(("dom", "row"), None),
        P(("dom", "row")),
        P(None, ("dom", "row")),
        P(None, ("dom", "row")),
        P(None, ("dom", "row")),
        P(None, ("dom", "row"), None),
        P(),
        P(),
        P(),
        P(),
        P(),
        P(),
        P(),
        P(),
    )
    out_specs = P(("dom", "row"), None)
    return jax.shard_map(shards, mesh=mesh, in_specs=in_specs, out_specs=out_specs, check_vma=False)
```

```python
import functools

import jax
import jax.numpy as jnp
from jax import lax
from jax.experimental import pallas as pl
from jax.experimental.pallas import tpu as pltpu
from jax.sharding import PartitionSpec as P

LANES = 128
F32 = jnp.float32
BF16 = jnp.bfloat16
I32 = jnp.int32
MIB = 1024 * 1024
VMEM_MIB = dict(plan=6, stage=6, codes=6, prep=16, serve=8, update=16)


def whole():
    return pl.BlockSpec(memory_space=pltpu.VMEM)


def call(kernel, out_shape, args, flops=0, name=None, specs=None, scalars=(), aliases=None):
    moved = sum(a.size * a.dtype.itemsize for a in args)
    moved += sum(o.size * o.dtype.itemsize for o in jax.tree.leaves(out_shape))
    specs = specs or {}
    return pl.pallas_call(
        kernel,
        out_shape=out_shape,
        grid_spec=pltpu.PrefetchScalarGridSpec(
            num_scalar_prefetch=len(scalars),
            grid=(1,) if scalars else (),
            in_specs=[specs.get(i, whole()) for i in range(len(args))],
            out_specs=jax.tree.map(lambda _: whole(), out_shape),
        ),
        input_output_aliases=aliases or {},
        compiler_params=pltpu.CompilerParams(vmem_limit_bytes=VMEM_MIB[name] * MIB),
        cost_estimate=pl.CostEstimate(flops=flops, bytes_accessed=moved, transcendentals=0),
        name=name,
    )(*scalars, *args)


def dot(a, b):
    return jnp.dot(a, b, preferred_element_type=F32)


def dot_nt(a, b):
    return lax.dot_general(a, b, (((1,), (1,)), ((), ())), preferred_element_type=F32)


def lane_code_f32(index_col, rows):
    lane = lax.broadcasted_iota(I32, (rows, LANES), 1)
    hit = (index_col & (LANES - 1)) == lane
    return jnp.where(hit, (index_col >> 7).astype(F32), -1.0)


def lane_code(index_col, rows):
    return lane_code_f32(index_col, rows).astype(BF16)


def expand(code, first, count):
    one = jnp.ones((), BF16)
    zero = jnp.zeros((), BF16)
    return jnp.concatenate(
        [jnp.where(code == jnp.asarray(k, BF16), one, zero) for k in range(first, first + count)],
        axis=1,
    )


def stage_kernel(_, *refs):
    count = len(refs) // 2
    for given, kept in zip(refs[:count], refs[count:]):
        kept[...] = given[...]


def plan_kernel(cap, ocap, node_dev, turn, owner_ref, me_ref, source_ref, ids_ref, pcode_ref):
    batches, events = source_ref.shape
    rows = ids_ref.shape[1]
    per = cap + ocap
    group_nodes = rows * node_dev
    upper = (
        lax.broadcasted_iota(I32, (events, events), 0)
        <= lax.broadcasted_iota(I32, (events, events), 1)
    ).astype(F32).astype(BF16)
    bucket_iota = lax.broadcasted_iota(I32, (2 * rows, events), 0)
    lane_iota = lax.broadcasted_iota(I32, (LANES, events), 0)
    high = jnp.zeros((rows, LANES), F32)
    low = jnp.zeros((rows, LANES), F32)
    places = []
    for b in range(batches):
        src = source_ref[b : b + 1, :]
        far = src >= group_nodes
        local = jnp.where(far, src - group_nodes, src)
        dest = local // node_dev
        offset = local - dest * node_dev
        bucket = jnp.where(far, dest + rows, dest)
        hit = bucket == bucket_iota
        hitf = hit.astype(F32)
        running = dot(hitf.astype(BF16), upper)
        rank = jnp.sum(hitf * running, axis=0, keepdims=True).astype(I32) - 1
        slot = jnp.where(far, rank + cap, rank)
        both = (hitf[:rows] + hitf[rows:]).astype(BF16)
        spot = (slot + b * per == lane_iota).astype(F32)
        high = high + dot_nt(both, (spot * (offset >> 6).astype(F32)).astype(BF16))
        low = low + dot_nt(both, (spot * (offset & 63).astype(F32)).astype(BF16))
        flip = jnp.where(((owner_ref[b] ^ me_ref[0]) & 1) == 0, 0, turn)
        places.append(jnp.where(far, dest ^ flip, dest) * per + slot)
    ids = high.astype(I32) * 64 + low.astype(I32)
    for g in range(ids_ref.shape[0]):
        ids_ref[g] = ids
    stacked = jnp.concatenate(
        [p.astype(F32) for p in places] + [jnp.zeros((LANES - batches, events), F32)], axis=0
    )
    cols = stacked.T
    for b in range(batches):
        pcode_ref[b] = lane_code(cols[:, b : b + 1].astype(I32), events)


def spread_codes(ids, first, count):
    rows = ids.shape[0]
    total = rows * count
    place = lax.broadcasted_iota(I32, (total, LANES), 0)
    lane = lax.broadcasted_iota(I32, (total, LANES), 1)
    row = place // count
    copy = (row[:, :rows] == lane[:, :rows]).astype(F32).astype(BF16)
    keep = (lane == first + place - row * count).astype(F32)
    ones = jnp.ones((LANES, LANES), BF16)

    def everywhere(part):
        taken = dot(copy, part.astype(F32).astype(BF16)) * keep
        return dot(taken.astype(BF16), ones)

    low = everywhere(ids & (LANES - 1))
    high = everywhere(ids >> 7)
    return jnp.where(low == lane.astype(F32), high, -1.0).astype(BF16)


def write_codes(b, me, cap, per, asked_ref, own_ref, far_ref):
    groups, rows, _ = asked_ref.shape
    own_ref[...] = spread_codes(asked_ref[me], b * per, per)
    block = rows * (per - cap)
    for g in range(groups):
        far_ref[g * block : (g + 1) * block, :] = spread_codes(
            asked_ref[g], b * per + cap, per - cap
        )


def code_kernel(cap, per, at_ref, asked_ref, own_ref, far_ref):
    write_codes(at_ref[0], at_ref[1], cap, per, asked_ref, own_ref, far_ref)


def cosine(x):
    turns = jnp.floor(x * 0.15915494309189535 + 0.5)
    r = (x - turns * 6.28125) - turns * 0.0019353071795864769
    z = r * r
    value = jnp.full_like(z, 1.0 / 20922789888000.0)
    for factor in (
        -1.0 / 87178291200.0,
        1.0 / 479001600.0,
        -1.0 / 3628800.0,
        1.0 / 40320.0,
        -1.0 / 720.0,
        1.0 / 24.0,
        -0.5,
        1.0,
    ):
        value = value * z + factor
    return value


def prep_kernel(
    width,
    cap,
    per,
    at_ref,
    table_ref,
    target_ref,
    time_ref,
    node_time_ref,
    edge_ref,
    freq_ref,
    phase_ref,
    w_ref,
    asked_ref,
    _,
    local_ref,
    scode_ref,
    same_ref,
    own_code_ref,
    far_code_ref,
):
    b = at_ref[0]
    write_codes(b + 1, at_ref[1], cap, per, asked_ref, own_code_ref, far_code_ref)
    batches, events = target_ref.shape
    node_dev = node_time_ref.shape[1]
    enc_at = 2 * width
    edge_at = enc_at + freq_ref.shape[1]
    trow = target_ref[pl.ds(b, 1), :]
    erow = time_ref[pl.ds(b, 1), :]
    stacked = jnp.concatenate(
        [trow.astype(F32), erow.astype(F32), jnp.zeros((LANES - 2, events), F32)], axis=0
    )
    cols = stacked.T
    sub = lax.broadcasted_iota(I32, (events, events), 0)
    lane = lax.broadcasted_iota(I32, (events, events), 1)
    node_lane = lax.broadcasted_iota(I32, (events, node_dev), 1)
    tcol = cols[:, 0:1].astype(I32)
    ecol = cols[:, 1:2]
    seen = jnp.max(
        jnp.where(tcol == node_lane, node_time_ref[...].astype(F32), 0.0), axis=1, keepdims=True
    )
    for before in range(batches - 1):
        row = target_ref[before : before + 1, :]
        row = jnp.where((row < 0) | (before >= b), -2, row)
        seen = jnp.maximum(
            seen,
            jnp.max(
                jnp.where(tcol == row, time_ref[before : before + 1, :].astype(F32), 0.0),
                axis=1,
                keepdims=True,
            ),
        )
    angle = (ecol - seen) * freq_ref[...] + phase_ref[...]
    encoded = cosine(angle).astype(BF16)
    mem = dot(expand(lane_code(tcol, events), 0, node_dev // LANES), table_ref[...])
    local_ref[:, :width] = (
        dot(encoded, w_ref[enc_at:edge_at, :])
        + dot(edge_ref[0], w_ref[edge_at:, :])
        + dot(mem.astype(BF16), w_ref[:width, :])
    )
    local_ref[:, width:] = mem
    same = (tcol == trow) & (trow >= 0)
    samef = same.astype(F32)
    same_ref[...] = samef.astype(BF16)
    earlier = jnp.max(jnp.where(sub < lane, samef, 0.0), axis=0, keepdims=True)
    first = jnp.where(earlier > 0.0, -1, trow)
    sub128 = lax.broadcasted_iota(I32, (LANES, events), 0)
    scode_ref[...] = jnp.where(
        (first & (LANES - 1)) == sub128, (first >> 7).astype(F32), -1.0
    ).astype(BF16)


def serve_rows(table_ref, code_ref, out_refs, step):
    blocks = table_ref.shape[0] // LANES
    table = table_ref[...]
    rows = out_refs[0].shape[0]
    for start in range(0, code_ref.shape[0], step):
        picked = dot(expand(code_ref[start : start + step, :], 0, blocks), table).astype(BF16)
        for part in range(0, step, rows):
            out_refs[(start + part) // rows][...] = picked[part : part + rows]


def serve_own_kernel(table_ref, own_code_ref, own_ref):
    halves = [own_ref.at[i : i + 512] for i in range(0, own_ref.shape[0], 512)]
    serve_rows(table_ref, own_code_ref, halves, 512)


def serve_far_kernel(table_ref, far_code_ref, *far_refs):
    serve_rows(table_ref, far_code_ref, far_refs, 512)


def update_kernel(
    last,
    at_ref,
    table_ref,
    back_ref,
    pcode_ref,
    local_ref,
    same_ref,
    scode_ref,
    w_ref,
    w_input_ref,
    w_hidden_ref,
    bias_input_ref,
    bias_hidden_ref,
    far_code_ref,
    new_ref,
    *far_out_refs,
):
    width = table_ref.shape[1]
    mem = local_ref[:, width:]
    hidden = dot(mem.astype(BF16), w_hidden_ref[...]) + bias_hidden_ref[...]
    source = dot(expand(pcode_ref[0], 0, back_ref.shape[0] // LANES), back_ref[...])
    w_source = w_ref[width : 2 * width, :]
    message = (local_ref[:, :width] + dot(source.astype(BF16), w_source)).astype(BF16)
    same = same_ref[...]
    total = dot(same, message)
    count = jnp.maximum(dot(same, jnp.ones((same.shape[0], LANES), BF16))[:, :1], 1.0)
    averaged = (total / count).astype(BF16)
    gates = dot(averaged, w_input_ref[...]) + bias_input_ref[...]
    reset = jax.nn.sigmoid(gates[:, :width] + hidden[:, :width])
    update = jax.nn.sigmoid(gates[:, width : 2 * width] + hidden[:, width : 2 * width])
    candidate = jnp.tanh(gates[:, 2 * width :] + reset * hidden[:, 2 * width :])
    fresh = ((1.0 - update) * candidate + update * mem).astype(BF16)
    ones = jnp.ones((fresh.shape[0], LANES), BF16)
    placed = jnp.concatenate([fresh, ones], axis=1)
    scode = scode_ref[...]
    one = jnp.ones((), BF16)
    zero = jnp.zeros((), BF16)
    blocks = table_ref.shape[0] // LANES
    group = 4
    for k in range(0, blocks, group):
        spread = jnp.concatenate(
            [jnp.where(scode == jnp.asarray(k + j, BF16), one, zero) for j in range(group)], axis=0
        )
        moved = dot(spread, placed)
        rows = slice(k * LANES, (k + group) * LANES)
        new_ref[rows, :] = jnp.where(
            moved[:, width : width + 1] > 0.0, moved[:, :width], table_ref[rows, :].astype(F32)
        ).astype(BF16)

    @pl.when(at_ref[0] < last)
    def _():
        serve_far_kernel(new_ref, far_code_ref, *far_out_refs)


def collect(table, own_code, far_rows, owner, turn, rows):
    width = table.shape[1]
    ys = len(far_rows) // 2

    def branch(root):
        y, z = root // 2, root % 2

        def body(table, own_code, *far_rows):
            me = lax.axis_index("dom")
            my_y, my_z = me >> 1, me & 1

            def spread(which):
                part = far_rows[2 * y + which]
                moved = []
                for shift in range(1, ys):
                    there = (y + shift) % ys
                    pairs = [(2 * y + side, 2 * there + side) for side in range(2)]
                    block = lax.ppermute(far_rows[2 * there + which], "dom", pairs)
                    moved.append((there, block))
                for there, block in moved:
                    part = jnp.where(my_y == there, block, part)
                return part

            own_rows = call(
                serve_own_kernel,
                jax.ShapeDtypeStruct((own_code.shape[0], width), BF16),
                (table, own_code),
                flops=2 * 10**9,
                name="serve",
            ).reshape(rows, -1, width)
            across = lax.ppermute(
                spread(1 - z),
                ("dom", "row"),
                [
                    ((2 * i + z) * rows + r, (2 * i + 1 - z) * rows + (r ^ turn))
                    for i in range(ys)
                    for r in range(rows)
                ],
            )
            mine = jnp.where(my_z == z, spread(z), across).reshape(rows, -1, width)
            return own_rows.at[:, own_rows.shape[1] - mine.shape[1] :, :].set(mine)

        return body

    return lax.switch(owner, [branch(r) for r in range(2 * ys)], table, own_code, *far_rows)


def shards(
    memory,
    node_time,
    target,
    source,
    event_time,
    edge_feat,
    owner_group,
    w_message,
    frequency,
    phase_shift,
    w_input,
    w_hidden,
    bias_input,
    bias_hidden,
):
    node_dev, width = memory.shape
    batches, events = target.shape
    rows = lax.axis_size("row")
    groups = lax.axis_size("dom")
    cap = 3 * events // (2 * rows)
    ocap = events // (2 * rows)
    per = cap + ocap
    shape = jax.ShapeDtypeStruct
    me = lax.axis_index("dom").astype(I32)
    turn = rows - rows // 4
    row_vectors = (
        node_time.reshape(1, node_dev),
        frequency.reshape(1, -1),
        phase_shift.reshape(1, -1),
    )
    input_row = bias_input.reshape(1, -1)
    hidden_row = bias_hidden.reshape(1, -1)
    anywhere = pl.BlockSpec(memory_space=pl.ANY)
    ids, pcode = call(
        functools.partial(plan_kernel, cap, ocap, node_dev, turn),
        (
            shape((groups, rows, batches * per), I32),
            shape((batches, events, LANES), BF16),
        ),
        (source,),
        name="plan",
        scalars=(owner_group, me.reshape(1)),
    )
    given = (memory,) + row_vectors
    table, times_row, freq_row, phase_row = call(
        stage_kernel,
        tuple(shape(v.shape, v.dtype) for v in given),
        (ids,) + given,
        flops=2 * 10**9,
        name="stage",
        specs={0: anywhere},
    )
    asked = lax.all_to_all(
        ids.reshape(groups * rows, 1, batches * per), ("dom", "row"), 0, 0, tiled=True
    ).reshape(groups, rows, batches * per)
    code_shapes = (
        shape((rows * per, LANES), BF16),
        shape((groups * rows * ocap, LANES), BF16),
    )
    own_code, far_code = call(
        functools.partial(code_kernel, cap, per),
        code_shapes,
        (asked,),
        flops=2 * 10**9,
        name="codes",
        scalars=(jnp.stack([jnp.zeros((), I32), me]),),
    )
    far_shape = (shape((rows * ocap, width), BF16),) * groups
    far_rows = call(
        serve_far_kernel, far_shape, (memory, far_code), flops=4 * 10**9, name="serve"
    )

    def batch(b, carry):
        owners, table, own_code, *far_rows = carry
        at = jnp.stack([b, me])
        sent = collect(
            table,
            own_code,
            far_rows,
            owners[0],
            turn,
            rows,
        )
        back = lax.all_to_all(sent, "row", 0, 0, tiled=True).reshape(rows * per, width)
        local, scode, same, next_own, next_far = call(
            functools.partial(prep_kernel, width, cap, per),
            (
                shape((events, 2 * width), F32),
                shape((LANES, events), BF16),
                shape((events, events), BF16),
            )
            + code_shapes,
            (table, target, event_time, times_row, edge_feat, freq_row, phase_row, w_message, asked, sent),
            flops=5 * 10**9,
            name="prep",
            specs={
                4: pl.BlockSpec((1,) + edge_feat.shape[1:], lambda i, at: (at[0], 0, 0)),
                9: anywhere,
            },
            scalars=(at,),
        )
        result = call(
            functools.partial(update_kernel, batches - 1),
            (shape((node_dev, width), BF16),) + far_shape,
            (
                table,
                back,
                pcode,
                local,
                same,
                scode,
                w_message,
                w_input,
                w_hidden,
                input_row,
                hidden_row,
                next_far,
            ),
            flops=6 * 10**9,
            name="update",
            specs={2: pl.BlockSpec((1, events, LANES), lambda i, at: (at[0], 0, 0))},
            scalars=(at,),
            aliases={1: 0},
        )
        return (owners[1:] + owners[:1], result[0], next_own) + tuple(result[1:])

    owners = tuple(owner_group[b] for b in range(batches))
    return lax.fori_loop(0, batches, batch, (owners, table, own_code, *far_rows))[1]


def solution(mesh):
    in_specs = (
        P(("dom", "row"), None),
        P(("dom", "row")),
        P(None, ("dom", "row")),
        P(None, ("dom", "row")),
        P(None, ("dom", "row")),
        P(None, ("dom", "row"), None),
        P(),
        P(),
        P(),
        P(),
        P(),
        P(),
        P(),
        P(),
    )
    out_specs = P(("dom", "row"), None)
    return jax.shard_map(shards, mesh=mesh, in_specs=in_specs, out_specs=out_specs, check_vma=False)
```

```python
import functools

import jax
import jax.numpy as jnp
from jax import lax
from jax.experimental import pallas as pl
from jax.experimental.pallas import tpu as pltpu
from jax.sharding import PartitionSpec as P

LANES = 128
F32 = jnp.float32
BF16 = jnp.bfloat16
I32 = jnp.int32
MIB = 1024 * 1024
VMEM_MIB = dict(plan=6, stage=6, codes=6, prep=16, serve=8, update=16)


def whole():
    return pl.BlockSpec(memory_space=pltpu.VMEM)


def call(kernel, out_shape, args, flops=0, name=None, specs=None, scalars=(), aliases=None):
    moved = sum(a.size * a.dtype.itemsize for a in args)
    moved += sum(o.size * o.dtype.itemsize for o in jax.tree.leaves(out_shape))
    specs = specs or {}
    return pl.pallas_call(
        kernel,
        out_shape=out_shape,
        grid_spec=pltpu.PrefetchScalarGridSpec(
            num_scalar_prefetch=len(scalars),
            grid=(1,) if scalars else (),
            in_specs=[specs.get(i, whole()) for i in range(len(args))],
            out_specs=jax.tree.map(lambda _: whole(), out_shape),
        ),
        input_output_aliases=aliases or {},
        compiler_params=pltpu.CompilerParams(vmem_limit_bytes=VMEM_MIB[name] * MIB),
        cost_estimate=pl.CostEstimate(flops=flops, bytes_accessed=moved, transcendentals=0),
        name=name,
    )(*scalars, *args)


def dot(a, b):
    return jnp.dot(a, b, preferred_element_type=F32)


def dot_nt(a, b):
    return lax.dot_general(a, b, (((1,), (1,)), ((), ())), preferred_element_type=F32)


def lane_code_f32(index_col, rows):
    lane = lax.broadcasted_iota(I32, (rows, LANES), 1)
    hit = (index_col & (LANES - 1)) == lane
    return jnp.where(hit, (index_col >> 7).astype(F32), -1.0)


def lane_code(index_col, rows):
    return lane_code_f32(index_col, rows).astype(BF16)


def expand(code, first, count):
    one = jnp.ones((), BF16)
    zero = jnp.zeros((), BF16)
    return jnp.concatenate(
        [jnp.where(code == jnp.asarray(k, BF16), one, zero) for k in range(first, first + count)],
        axis=1,
    )


def stage_kernel(_, *refs):
    count = len(refs) // 2
    for given, kept in zip(refs[:count], refs[count:]):
        kept[...] = given[...]


def plan_kernel(cap, ocap, node_dev, flip_ref, source_ref, ids_ref, pcode_ref):
    batches, events = source_ref.shape
    rows = ids_ref.shape[1]
    per = cap + ocap
    group_nodes = rows * node_dev
    upper = (
        lax.broadcasted_iota(I32, (events, events), 0)
        <= lax.broadcasted_iota(I32, (events, events), 1)
    ).astype(F32).astype(BF16)
    bucket_iota = lax.broadcasted_iota(I32, (2 * rows, events), 0)
    lane_iota = lax.broadcasted_iota(I32, (LANES, events), 0)
    high = jnp.zeros((rows, LANES), F32)
    low = jnp.zeros((rows, LANES), F32)
    places = []
    for b in range(batches):
        src = source_ref[b : b + 1, :]
        far = src >= group_nodes
        local = jnp.where(far, src - group_nodes, src)
        dest = local // node_dev
        offset = local - dest * node_dev
        bucket = jnp.where(far, dest + rows, dest)
        hit = bucket == bucket_iota
        hitf = hit.astype(F32)
        running = dot(hitf.astype(BF16), upper)
        rank = jnp.sum(hitf * running, axis=0, keepdims=True).astype(I32) - 1
        slot = jnp.where(far, rank + cap, rank)
        both = (hitf[:rows] + hitf[rows:]).astype(BF16)
        spot = (slot + b * per == lane_iota).astype(F32)
        high = high + dot_nt(both, (spot * (offset >> 6).astype(F32)).astype(BF16))
        low = low + dot_nt(both, (spot * (offset & 63).astype(F32)).astype(BF16))
        places.append(jnp.where(far, dest ^ flip_ref[b], dest) * per + slot)
    ids = high.astype(I32) * 64 + low.astype(I32)
    for g in range(ids_ref.shape[0]):
        ids_ref[g] = ids
    stacked = jnp.concatenate(
        [p.astype(F32) for p in places] + [jnp.zeros((LANES - batches, events), F32)], axis=0
    )
    cols = stacked.T
    for b in range(batches):
        pcode_ref[b] = lane_code(cols[:, b : b + 1].astype(I32), events)


def spread_codes(ids, first, count):
    rows = ids.shape[0]
    total = rows * count
    place = lax.broadcasted_iota(I32, (total, LANES), 0)
    lane = lax.broadcasted_iota(I32, (total, LANES), 1)
    row = place // count
    copy = (row[:, :rows] == lane[:, :rows]).astype(F32).astype(BF16)
    keep = (lane == first + place - row * count).astype(F32)
    ones = jnp.ones((LANES, LANES), BF16)

    def everywhere(part):
        taken = dot(copy, part.astype(F32).astype(BF16)) * keep
        return dot(taken.astype(BF16), ones)

    low = everywhere(ids & (LANES - 1))
    high = everywhere(ids >> 7)
    return jnp.where(low == lane.astype(F32), high, -1.0).astype(BF16)


def write_codes(b, me, cap, per, asked_ref, own_ref, far_ref):
    groups, rows, _ = asked_ref.shape
    own_ref[...] = spread_codes(asked_ref[me], b * per, per)
    block = rows * (per - cap)
    for g in range(groups):
        far_ref[g * block : (g + 1) * block, :] = spread_codes(
            asked_ref[g], b * per + cap, per - cap
        )


def code_kernel(cap, per, at_ref, asked_ref, own_ref, far_ref):
    write_codes(at_ref[0], at_ref[1], cap, per, asked_ref, own_ref, far_ref)


def cosine(x):
    turns = jnp.floor(x * 0.15915494309189535 + 0.5)
    r = (x - turns * 6.28125) - turns * 0.0019353071795864769
    z = r * r
    value = jnp.full_like(z, 1.0 / 20922789888000.0)
    for factor in (
        -1.0 / 87178291200.0,
        1.0 / 479001600.0,
        -1.0 / 3628800.0,
        1.0 / 40320.0,
        -1.0 / 720.0,
        1.0 / 24.0,
        -0.5,
        1.0,
    ):
        value = value * z + factor
    return value


def prep_kernel(
    width,
    cap,
    per,
    at_ref,
    table_ref,
    target_ref,
    time_ref,
    node_time_ref,
    edge_ref,
    freq_ref,
    phase_ref,
    w_ref,
    asked_ref,
    _,
    local_ref,
    scode_ref,
    same_ref,
    own_code_ref,
    far_code_ref,
):
    b = at_ref[0]
    write_codes(b + 1, at_ref[1], cap, per, asked_ref, own_code_ref, far_code_ref)
    batches, events = target_ref.shape
    node_dev = node_time_ref.shape[1]
    enc_at = 2 * width
    edge_at = enc_at + freq_ref.shape[1]
    trow = target_ref[pl.ds(b, 1), :]
    erow = time_ref[pl.ds(b, 1), :]
    stacked = jnp.concatenate(
        [trow.astype(F32), erow.astype(F32), jnp.zeros((LANES - 2, events), F32)], axis=0
    )
    cols = stacked.T
    sub = lax.broadcasted_iota(I32, (events, events), 0)
    lane = lax.broadcasted_iota(I32, (events, events), 1)
    node_lane = lax.broadcasted_iota(I32, (events, node_dev), 1)
    tcol = cols[:, 0:1].astype(I32)
    ecol = cols[:, 1:2]
    seen = jnp.max(
        jnp.where(tcol == node_lane, node_time_ref[...].astype(F32), 0.0), axis=1, keepdims=True
    )
    for before in range(batches - 1):
        row = target_ref[before : before + 1, :]
        row = jnp.where((row < 0) | (before >= b), -2, row)
        seen = jnp.maximum(
            seen,
            jnp.max(
                jnp.where(tcol == row, time_ref[before : before + 1, :].astype(F32), 0.0),
                axis=1,
                keepdims=True,
            ),
        )
    angle = (ecol - seen) * freq_ref[...] + phase_ref[...]
    encoded = cosine(angle).astype(BF16)
    mem = dot(expand(lane_code(tcol, events), 0, node_dev // LANES), table_ref[...])
    local_ref[:, :width] = (
        dot(encoded, w_ref[enc_at:edge_at, :])
        + dot(edge_ref[0], w_ref[edge_at:, :])
        + dot(mem.astype(BF16), w_ref[:width, :])
    )
    local_ref[:, width:] = mem
    same = (tcol == trow) & (trow >= 0)
    samef = same.astype(F32)
    same_ref[...] = samef.astype(BF16)
    earlier = jnp.max(jnp.where(sub < lane, samef, 0.0), axis=0, keepdims=True)
    first = jnp.where(earlier > 0.0, -1, trow)
    sub128 = lax.broadcasted_iota(I32, (LANES, events), 0)
    scode_ref[...] = jnp.where(
        (first & (LANES - 1)) == sub128, (first >> 7).astype(F32), -1.0
    ).astype(BF16)


def serve_rows(table_ref, code_ref, out_refs, step):
    blocks = table_ref.shape[0] // LANES
    table = table_ref[...]
    rows = out_refs[0].shape[0]
    for start in range(0, code_ref.shape[0], step):
        picked = dot(expand(code_ref[start : start + step, :], 0, blocks), table).astype(BF16)
        for part in range(0, step, rows):
            out_refs[(start + part) // rows][...] = picked[part : part + rows]


def serve_own_kernel(table_ref, own_code_ref, own_ref):
    halves = [own_ref.at[i : i + 512] for i in range(0, own_ref.shape[0], 512)]
    serve_rows(table_ref, own_code_ref, halves, 512)


def serve_far_kernel(table_ref, far_code_ref, *far_refs):
    serve_rows(table_ref, far_code_ref, far_refs, 512)


def update_kernel(
    last,
    at_ref,
    table_ref,
    back_ref,
    pcode_ref,
    local_ref,
    same_ref,
    scode_ref,
    w_ref,
    w_input_ref,
    w_hidden_ref,
    bias_input_ref,
    bias_hidden_ref,
    far_code_ref,
    new_ref,
    *far_out_refs,
):
    width = table_ref.shape[1]
    mem = local_ref[:, width:]
    hidden = dot(mem.astype(BF16), w_hidden_ref[...]) + bias_hidden_ref[...]
    source = dot(expand(pcode_ref[0], 0, back_ref.shape[0] // LANES), back_ref[...])
    w_source = w_ref[width : 2 * width, :]
    message = (local_ref[:, :width] + dot(source.astype(BF16), w_source)).astype(BF16)
    same = same_ref[...]
    total = dot(same, message)
    count = jnp.maximum(dot(same, jnp.ones((same.shape[0], LANES), BF16))[:, :1], 1.0)
    averaged = (total / count).astype(BF16)
    gates = dot(averaged, w_input_ref[...]) + bias_input_ref[...]
    reset = jax.nn.sigmoid(gates[:, :width] + hidden[:, :width])
    update = jax.nn.sigmoid(gates[:, width : 2 * width] + hidden[:, width : 2 * width])
    candidate = jnp.tanh(gates[:, 2 * width :] + reset * hidden[:, 2 * width :])
    fresh = ((1.0 - update) * candidate + update * mem).astype(BF16)
    ones = jnp.ones((fresh.shape[0], LANES), BF16)
    placed = jnp.concatenate([fresh, ones], axis=1)
    scode = scode_ref[...]
    one = jnp.ones((), BF16)
    zero = jnp.zeros((), BF16)
    blocks = table_ref.shape[0] // LANES
    group = 4
    for k in range(0, blocks, group):
        spread = jnp.concatenate(
            [jnp.where(scode == jnp.asarray(k + j, BF16), one, zero) for j in range(group)], axis=0
        )
        moved = dot(spread, placed)
        rows = slice(k * LANES, (k + group) * LANES)
        new_ref[rows, :] = jnp.where(
            moved[:, width : width + 1] > 0.0, moved[:, :width], table_ref[rows, :].astype(F32)
        ).astype(BF16)

    @pl.when(at_ref[0] < last)
    def _():
        serve_far_kernel(new_ref, far_code_ref, *far_out_refs)


def collect(table, own_code, far_rows, owner, turn, rows):
    width = table.shape[1]
    ys = len(far_rows) // 2

    def branch(root):
        y, z = root // 2, root % 2

        def body(table, own_code, *far_rows):
            me = lax.axis_index("dom")
            my_y, my_z = me >> 1, me & 1

            def spread(which):
                part = far_rows[2 * y + which]
                moved = []
                for shift in sorted(range(1, ys), key=lambda k: -min(k, ys - k)):
                    there = (y + shift) % ys
                    pairs = [(2 * y + side, 2 * there + side) for side in range(2)]
                    block = lax.ppermute(far_rows[2 * there + which], "dom", pairs)
                    moved.append((there, block))
                for there, block in moved:
                    part = jnp.where(my_y == there, block, part)
                return part

            own_rows = call(
                serve_own_kernel,
                jax.ShapeDtypeStruct((own_code.shape[0], width), BF16),
                (table, own_code),
                flops=2 * 10**9,
                name="serve",
            ).reshape(rows, -1, width)
            across = lax.ppermute(
                spread(1 - z),
                ("dom", "row"),
                [
                    ((2 * i + z) * rows + r, (2 * i + 1 - z) * rows + (r ^ turn))
                    for i in range(ys)
                    for r in range(rows)
                ],
            )
            mine = jnp.where(my_z == z, spread(z), across).reshape(rows, -1, width)
            return own_rows.at[:, own_rows.shape[1] - mine.shape[1] :, :].set(mine)

        return body

    return lax.switch(owner, [branch(r) for r in range(2 * ys)], table, own_code, *far_rows)


def shards(
    memory,
    node_time,
    target,
    source,
    event_time,
    edge_feat,
    owner_group,
    w_message,
    frequency,
    phase_shift,
    w_input,
    w_hidden,
    bias_input,
    bias_hidden,
):
    node_dev, width = memory.shape
    batches, events = target.shape
    rows = lax.axis_size("row")
    groups = lax.axis_size("dom")
    cap = 3 * events // (2 * rows)
    ocap = events // (2 * rows)
    per = cap + ocap
    shape = jax.ShapeDtypeStruct
    me = lax.axis_index("dom").astype(I32)
    turn = rows - rows // 4
    flip = jnp.where((owner_group & 1) == (me & 1), 0, turn).astype(I32)
    row_vectors = (
        node_time.reshape(1, node_dev),
        frequency.reshape(1, -1),
        phase_shift.reshape(1, -1),
    )
    input_row = bias_input.reshape(1, -1)
    hidden_row = bias_hidden.reshape(1, -1)
    anywhere = pl.BlockSpec(memory_space=pl.ANY)
    ids, pcode = call(
        functools.partial(plan_kernel, cap, ocap, node_dev),
        (
            shape((groups, rows, batches * per), I32),
            shape((batches, events, LANES), BF16),
        ),
        (source,),
        name="plan",
        scalars=(flip,),
    )
    given = (memory,) + row_vectors
    table, times_row, freq_row, phase_row = call(
        stage_kernel,
        tuple(shape(v.shape, v.dtype) for v in given),
        (ids,) + given,
        flops=2 * 10**9,
        name="stage",
        specs={0: anywhere},
    )
    asked = lax.all_to_all(
        ids.reshape(groups * rows, 1, batches * per), ("dom", "row"), 0, 0, tiled=True
    ).reshape(groups, rows, batches * per)
    code_shapes = (
        shape((rows * per, LANES), BF16),
        shape((groups * rows * ocap, LANES), BF16),
    )
    own_code, far_code = call(
        functools.partial(code_kernel, cap, per),
        code_shapes,
        (asked,),
        flops=2 * 10**9,
        name="codes",
        scalars=(jnp.stack([jnp.zeros((), I32), me]),),
    )
    far_shape = (shape((rows * ocap, width), BF16),) * groups
    far_rows = call(
        serve_far_kernel, far_shape, (memory, far_code), flops=4 * 10**9, name="serve"
    )

    def batch(b, carry):
        table, own_code, *far_rows = carry
        at = jnp.stack([b, me])
        sent = collect(
            table,
            own_code,
            far_rows,
            lax.dynamic_index_in_dim(owner_group, b, 0, keepdims=False),
            turn,
            rows,
        )
        back = lax.all_to_all(sent, "row", 0, 0, tiled=True).reshape(rows * per, width)
        local, scode, same, next_own, next_far = call(
            functools.partial(prep_kernel, width, cap, per),
            (
                shape((events, 2 * width), F32),
                shape((LANES, events), BF16),
                shape((events, events), BF16),
            )
            + code_shapes,
            (table, target, event_time, times_row, edge_feat, freq_row, phase_row, w_message, asked, sent),
            flops=5 * 10**9,
            name="prep",
            specs={
                4: pl.BlockSpec((1,) + edge_feat.shape[1:], lambda i, at: (at[0], 0, 0)),
                9: anywhere,
            },
            scalars=(at,),
        )
        result = call(
            functools.partial(update_kernel, batches - 1),
            (shape((node_dev, width), BF16),) + far_shape,
            (
                table,
                back,
                pcode,
                local,
                same,
                scode,
                w_message,
                w_input,
                w_hidden,
                input_row,
                hidden_row,
                next_far,
            ),
            flops=6 * 10**9,
            name="update",
            specs={2: pl.BlockSpec((1, events, LANES), lambda i, at: (at[0], 0, 0))},
            scalars=(at,),
            aliases={1: 0},
        )
        return (result[0], next_own) + tuple(result[1:])

    return lax.fori_loop(0, batches, batch, (table, own_code, *far_rows))[0]


def solution(mesh):
    in_specs = (
        P(("dom", "row"), None),
        P(("dom", "row")),
        P(None, ("dom", "row")),
        P(None, ("dom", "row")),
        P(None, ("dom", "row")),
        P(None, ("dom", "row"), None),
        P(),
        P(),
        P(),
        P(),
        P(),
        P(),
        P(),
        P(),
    )
    out_specs = P(("dom", "row"), None)
    return jax.shard_map(shards, mesh=mesh, in_specs=in_specs, out_specs=out_specs, check_vma=False)
```
